256 devices in a mesh: section: 8 (over y, core), rows: 32 (over x, z).
Axes of the slice: x: 4, y: 4, z: 8, core: 2. Of those that a mesh axis runs over, the one named last changes fastest.
Arguments:
- grad_in: bfloat16 [8, 8192, 256], P('section', 'rows'), may hold values from -6 to 6
- grad_last: bfloat16 [8192, 256], P('rows'), may hold values from -6 to 6
- support: bfloat16 [8, 2, 2, 8192, 256], P('section', None, None, 'rows'), may hold values from -6 to 6
- preact: bfloat16 [8, 2, 2, 8192, 256], P('section', None, None, 'rows'), may hold values from -6 to 6
- weights: bfloat16 [8, 2, 256, 256], P('section'), may hold values from -0.375 to 0.375
- tile_vals: bfloat16 [8, 2, 3072, 128, 128], P('section', None, 'rows'), may hold values from -0.078125 to 0.078125
- tile_row: int32 [8, 2, 3072], P('section', None, 'rows'), may hold values from 0 to 1
- tile_col: int32 [8, 2, 3072], P('section', None, 'rows'), may hold values from 0 to 63, as said below
- tile_count: int32 [8, 2, 32], P('section', None, 'rows'), may hold values from 48 to 96, as said below
Outputs:
- handoff: bfloat16 [2, 8, 8192, 256], P(None, 'section', 'rows')
- init_grad: float32 [8, 2, 8192, 256], P('section', None, 'rows')
- weight_grad: float32 [8, 2, 256, 256], P('section')
The draws below stay inside these ranges and needn't reach their ends.
Inputs may be any that keep to these rules, and one draw needn't show every extreme that they name: tile_count[s, t, d] is the number of live entries in device d's list; in every section and micro-batch some device has all 96 live. `tile_col`: for every section, micro-batch and pair of devices d and o with o != d, all entries of device d's list (live or padding) whose column tile lies in device o's rows name one and the same of o's 2 row tiles.
All inputs are finite; a program needn't handle non-finite values.
Results may differ from the reference program's by a relative error of at most 0.0066.
Values may be sent and summed in bfloat16 or wider, within the bound.
A program may use at most 128 MiB of HBM per device.

```python
import jax
import jax.numpy as jnp
from jax import lax

WIDTH = 256
TILE = 128
LAYERS = 2
TICKS = 2
TILES_DEV = 96
SECTIONS = 8
SHARDS = 32
NODES = 8192
BLOCKS = 64
ROW_TILES = 2
TILES = 3072


def draw_tile_count(key, part):
    first, second = jax.random.split(jax.random.fold_in(key, 17))
    base = TILES_DEV - jax.random.randint(first, (SECTIONS, TICKS, SHARDS), 0, TILES_DEV // 2 + 1)
    picked = jax.random.randint(second, (SECTIONS, TICKS, 1), 0, SHARDS)
    full = jnp.arange(SHARDS)[None, None, :] == picked
    return jnp.where(full, TILES_DEV, base).astype(jnp.int32)


def draw_tile_col(key, part):
    keys = jax.random.split(jax.random.fold_in(key, 29), 5)
    allowed = jax.random.randint(keys[0], (SECTIONS, TICKS, SHARDS, SHARDS), 0, ROW_TILES)
    device = (jnp.arange(TILES) // TILES_DEV).astype(jnp.int32)
    kinds = jax.random.randint(keys[1], (SECTIONS, TICKS, TILES), 0, 4)
    sideways = 2 * jax.random.randint(keys[2], (SECTIONS, TICKS, TILES), 0, 2) - 1
    far_step = jax.random.randint(keys[3], (SECTIONS, TICKS, TILES), 1, SHARDS)
    own_block = jax.random.randint(keys[4], (SECTIONS, TICKS, TILES), 0, ROW_TILES)
    near_owner = (device[None, None, :] + sideways) % SHARDS
    far_owner = (device[None, None, :] + far_step) % SHARDS
    owners = jnp.where(kinds < 2, device[None, None, :], jnp.where(kinds == 2, near_owner, far_owner)).astype(jnp.int32)
    rows_of = allowed[:, :, device, :]
    remote_block = jnp.take_along_axis(rows_of, owners[..., None], axis=-1)[..., 0]
    block = jnp.where(kinds < 2, own_block, remote_block)
    return (owners * ROW_TILES + block).astype(jnp.int32)


def with_ends(result, stream_key, smallest, high):
    shape = result.shape
    index_at = [jax.random.randint(jax.random.fold_in(stream_key, axis), (), 0, shape[axis]) for axis in range(len(shape))]
    result = result.at[tuple(index_at)].set(smallest)
    longest = shape.index(max(shape))
    index_at[longest] = (index_at[longest] + 1) % shape[longest]
    return result.at[tuple(index_at)].set(high)


def shard_levels(stream_key, extent, pieces, smallest, largest):
    def one(dim, parts):
        steps = jax.random.uniform(jax.random.fold_in(jax.random.fold_in(stream_key, 6), dim), (parts,), jnp.float32, smallest / len(pieces), largest / len(pieces))
        return jnp.repeat(jnp.exp(steps), extent[dim] // parts).reshape((-1,) + (1,) * (len(extent) - dim - 1))

    loudness = one(*pieces[0])
    for cut in pieces[1:]:
        loudness = loudness * one(*cut)
    return loudness


def noise(stream_key, dims, scale, most, pieces=(), held_as=jnp.bfloat16):
    result = scale * jax.random.normal(stream_key, dims, jnp.float32)
    if pieces:
        result = result * shard_levels(stream_key, dims, pieces, -0.22, 0.18)
    return jnp.clip(result, -most, most).astype(held_as)


def setup_inputs(seed: int = 0) -> dict:
    arg_keys = jax.random.split(jax.random.key(seed), 10)
    grad_in = noise(arg_keys[0], (SECTIONS, NODES, WIDTH), 1.0, 6.0, ((0, 8), (1, 32)))
    grad_last = noise(arg_keys[1], (NODES, WIDTH), 1.0, 6.0, ((0, 32),))
    support = noise(arg_keys[2], (SECTIONS, TICKS, LAYERS, NODES, WIDTH), 1.0, 6.0, ((0, 8), (3, 32)))
    preact = noise(arg_keys[3], (SECTIONS, TICKS, LAYERS, NODES, WIDTH), 1.0, 6.0, ((0, 8), (3, 32)))
    weights = noise(arg_keys[4], (SECTIONS, LAYERS, WIDTH, WIDTH), WIDTH ** -0.5, 0.375, ((0, 8),))
    tile_vals = noise(arg_keys[5], (SECTIONS, TICKS, TILES, TILE, TILE), (TILE * TILES_DEV // ROW_TILES) ** -0.5, 0.078125, ((0, 8), (2, 32)))
    tile_row = with_ends(jax.random.randint(arg_keys[6], (SECTIONS, TICKS, TILES), 0, ROW_TILES), jax.random.fold_in(arg_keys[6], 1), 0, ROW_TILES - 1).astype(jnp.int32)
    tile_col = draw_tile_col(jax.random.fold_in(arg_keys[9], 71), 0)
    tile_count = draw_tile_count(jax.random.fold_in(arg_keys[9], 71), 0)
    return dict(grad_in=grad_in, grad_last=grad_last, support=support, preact=preact, weights=weights, tile_vals=tile_vals, tile_row=tile_row, tile_col=tile_col, tile_count=tile_count)


ALPHA = 0.1
BETA_SCALE = 0.5


def tile_product(dense, values, row_local, cols, counts):
    blocks = dense.astype(jnp.float32).reshape(BLOCKS, TILE, WIDTH)[cols]
    products = jnp.einsum("kab,kbf->kaf", values.astype(jnp.float32), blocks, precision=lax.Precision.HIGHEST)
    owner = (jnp.arange(TILES) // TILES_DEV).astype(jnp.int32)
    live = (jnp.arange(TILES) % TILES_DEV) < counts[owner]
    products = products * live.astype(jnp.float32)[:, None, None]
    row_global = (owner * ROW_TILES + row_local).astype(jnp.int32)
    summed = jax.ops.segment_sum(products, row_global, num_segments=BLOCKS)
    return summed.reshape(NODES, WIDTH)


def reference(grad_in, grad_last, support, preact, weights, tile_vals, tile_row, tile_col, tile_count):
    weight_acc = [[jnp.zeros((WIDTH, WIDTH), jnp.float32) for layer in range(LAYERS)] for section in range(SECTIONS)]
    handoff = []
    initial = []
    previous = None
    for tick in range(TICKS):
        outs_now = []
        init_now = []
        for section in range(SECTIONS):
            if tick == 0:
                grad = grad_in[section]
            elif section == SECTIONS - 1:
                grad = grad_last
            else:
                grad = previous[section + 1]
            toward = jnp.zeros((NODES, WIDTH), jnp.float32)
            for layer in reversed(range(LAYERS)):
                beta = jnp.log(BETA_SCALE / jnp.asarray(LAYERS * section + layer + 1, jnp.float32) + 1.0)
                weight = weights[section, layer]
                masked = jnp.where(preact[section, tick, layer] > 0, grad, jnp.zeros_like(grad))
                term = beta * jnp.dot(support[section, tick, layer].T, masked, preferred_element_type=jnp.float32)
                weight_acc[section][layer] = weight_acc[section][layer] + term
                image = ((1.0 - beta) * masked.astype(jnp.float32) + beta * jnp.dot(masked, weight.T, preferred_element_type=jnp.float32)).astype(jnp.bfloat16)
                toward = toward + ALPHA * image.astype(jnp.float32)
                spread = tile_product(image, tile_vals[section, tick], tile_row[section, tick], tile_col[section, tick], tile_count[section, tick])
                grad = ((1.0 - ALPHA) * spread).astype(jnp.bfloat16)
            outs_now.append(grad)
            init_now.append(toward)
        previous = outs_now
        handoff.append(jnp.stack(outs_now))
        initial.append(jnp.stack(init_now))
    weight_grad = jnp.stack([jnp.stack(weight_acc[section]) for section in range(SECTIONS)])
    return jnp.stack(handoff), jnp.stack(initial, axis=1), weight_grad
```

```python
import jax
import jax.numpy as jnp
from jax import lax
from jax.experimental import pallas as pl
from jax.experimental.pallas import tpu as pltpu
from jax.sharding import PartitionSpec as P

ALPHA = 0.1
BETA_SCALE = 0.5
MESH = pl.DeviceIdType.MESH

SECTIONS = 8
XS = 4
ZS = 8
TILE = 128
WIDTH = 256
ROWS = 256
LIST = 96
CHUNKS = 24
F32 = jnp.float32
BF16 = jnp.bfloat16
I32 = jnp.int32


def kernel(
    grad_in, grad_last, support, preact, weights, vals_hbm, row_in, col_in, count_in,
    hand_out, init_out, wg_out,
    wg_acc, x_part, x_in, z_own, z_part, z_in, z_done, x_done,
    vals, key_buf, tab_v, tab_s, need, need_m, need_p, run, dense,
    full, half, pick, grad_buf, masked_buf, acc, handed,
    vals_sem, tab_sem, need_send, need_recv, full_send, full_recv, half_send, half_recv,
    hand_send, hand_recv, sum_xs, sum_xr, sum_zs, sum_zr, fin_zs, fin_zr, fin_xs, fin_xr,
):
    section = lax.axis_index("section")
    me = lax.axis_index("rows")
    x = me // ZS
    z = me % ZS

    def at(sec, xx, zz):
        return (sec, xx * ZS + zz)

    x_up = at(section, (x + 1) % XS, z)
    x_dn = at(section, (x + XS - 1) % XS, z)
    z_up = at(section, x, (z + 1) % ZS)
    z_dn = at(section, x, (z + ZS - 1) % ZS)
    s_up = at((section + 1) % SECTIONS, x, z)
    s_dn = at((section + SECTIONS - 1) % SECTIONS, x, z)

    for t in range(2):
        pltpu.make_async_copy(vals_hbm.at[0, t], vals.at[t], vals_sem.at[t]).start()

    barrier = pltpu.get_barrier_semaphore()
    across_x = [at(section, (x + d) % XS, z) for d in range(1, XS)]
    across_z = [at(section, x, (z + d) % ZS) for d in range(1, ZS)]
    peers = across_x + across_z + [s_up, s_dn]
    for peer in peers:
        pl.semaphore_signal(barrier, inc=1, device_id=peer, device_id_type=MESH)

    def remote(src, dst, send, recv, device):
        return pltpu.make_async_remote_copy(
            src_ref=src, dst_ref=dst, send_sem=send, recv_sem=recv,
            device_id=device, device_id_type=MESH,
        )

    def tile(h):
        return pl.ds(h * TILE, TILE)

    def send_up(i, c, k, h):
        k_to = (k + 7) % ZS
        return remote(
            full.at[i, c, k, tile(h)], full.at[i, c, k_to, tile(h)],
            full_send.at[0, c, k, h], full_recv.at[i, c, k_to, h], z_up,
        )

    def send_dn(i, c, k, h):
        k_to = (k + 1) % ZS
        return remote(
            full.at[i, c, k, tile(h)], full.at[i, c, k_to, tile(h)],
            full_send.at[1, c, k, h], full_recv.at[i, c, k_to, h], z_dn,
        )

    def send_side(i, h):
        return remote(
            full.at[i, 0, 0, tile(h)], full.at[i, 1, 0, tile(h)],
            full_send.at[2, 0, 0, h], full_recv.at[i, 1, 0, h], x_up,
        )

    def send_pick(i, c, k):
        return remote(
            pick.at[c, k], half.at[i, k, tile(c)],
            half_send.at[c, k], half_recv.at[i, c, k], x_dn if c == 0 else x_up,
        )

    def got_full(i, c, k, h):
        remote(
            full.at[i, c, k, tile(h)], full.at[i, c, k, tile(h)],
            full_send.at[0, c, k, h], full_recv.at[i, c, k, h], z_up,
        ).wait_recv()

    def got_half(i, c, k):
        remote(
            pick.at[c, k], half.at[i, k, tile(c)],
            half_send.at[c, k], half_recv.at[i, c, k], x_up,
        ).wait_recv()

    need_copies = [
        remote(need, need_m, need_send.at[0], need_recv.at[0], x_up),
        remote(need, need_p, need_send.at[1], need_recv.at[1], x_dn),
    ]

    def all_sends(i):
        copies = []
        for c in range(2):
            for k in (0, 7, 6):
                copies += [send_up(i, c, k, 0), send_up(i, c, k, 1)]
            copies.append(send_up(i, c, 5, 0))
            for k in (0, 1, 2):
                copies += [send_dn(i, c, k, 0), send_dn(i, c, k, 1)]
            copies.append(send_dn(i, c, 3, 1))
        copies += [send_side(i, 0), send_side(i, 1)]
        for c in range(2):
            for k in range(ZS):
                copies.append(send_pick(i, c, k))
        return copies

    def beta_of(layer):
        depth = (2 * section + layer + 1).astype(F32)
        return jnp.log(BETA_SCALE / jnp.full((8, 128), depth, F32) + 1.0)[0:1, 0:1]

    def find_needs():
        slot = lax.broadcasted_iota(I32, (16, LIST), 0)
        far = jnp.where(slot < 8, (x + 1) % XS, (x + 2) % XS)
        owner = far * ZS + (z + slot) % ZS
        for t in range(2):
            col = jnp.broadcast_to(col_in[0, t : t + 1, :], (16, LIST))
            second = jnp.where((col >> 1) == owner, (col & 1).astype(F32), 0.0)
            need[t * 16 : (t + 1) * 16, :] = jnp.broadcast_to(
                jnp.max(second, axis=1, keepdims=True), (16, 128)
            )

    def sort_entries(t):
        col = col_in[0, pl.ds(t, 1), :]
        owner = col >> 1
        dx = ((owner >> 3) - x) & 3
        dz = ((owner & 7) - z) & 7
        near = (dx == 0) | (dx == 3)
        chunk = jnp.where(near, jnp.where(dx == 3, 8 + dz, dz), 16 + dz)
        side = jnp.where(near, col & 1, dx - 1)
        key = chunk * 4 + side * 2 + row_in[0, pl.ds(t, 1), :]
        place = lax.broadcasted_iota(I32, (1, LIST), 1)
        key = jnp.where(place < count_in[0, pl.ds(t, 1), :], key, 127)
        key_buf[...] = jnp.full((8, 128), 127, I32)
        key_buf[0:1, 0:LIST] = key
        across = jnp.broadcast_to(key_buf[0:1, :], (128, 128))
        down = across.T
        lane = lax.broadcasted_iota(I32, (128, 128), 1)
        sub = lax.broadcasted_iota(I32, (128, 128), 0)

        def count(hit, axis):
            return jnp.sum(jnp.where(hit, 1, 0), axis=axis, keepdims=True)

        rank = count((across < down) | ((across == down) & (lane < sub)), 1)

        def pull(values, position):
            return jnp.sum(jnp.where(rank == position, values, 0), axis=0, keepdims=True)

        order = pull(sub, lane)
        same = jnp.where(
            (pull(down, lane) == pull(down, lane - 1)) & (lane[0:1, :] > 0), 1, 0
        )
        last = jnp.maximum(count(down <= lane, 0) - 1, 0)
        there = jnp.where(count(down == lane, 0) > 0, 1, 0)
        for r, line in enumerate((order, same, last, there)):
            tab_v[r : r + 1, :] = line
        fetch = pltpu.make_async_copy(tab_v, tab_s, tab_sem)
        fetch.start()
        fetch.wait()

    def build_dense(t):
        sort_entries(t)

        @pl.when(t == 0)
        def _():
            for u in range(2):
                pltpu.make_async_copy(vals_hbm.at[0, u], vals.at[u], vals_sem.at[u]).wait()

        def add(e, total):
            total = total * tab_s[1, e].astype(F32) + vals[t, tab_s[0, e]].astype(F32)
            run[e] = total
            return total

        lax.fori_loop(0, LIST, add, jnp.zeros((TILE, TILE), F32), unroll=4)

        def fill(j, carry):
            for side in range(2):
                for r in range(2):
                    slot = j * 4 + side * 2 + r
                    value = run[tab_s[2, slot]] * tab_s[3, slot].astype(F32)
                    dense[t, j, tile(r), tile(side)] = value.astype(BF16)
            return carry

        lax.fori_loop(0, CHUNKS, fill, 0)

    def sum_x(w, d):
        return remote(
            x_part.at[w, (x + d) % XS], x_in.at[w, d - 1],
            sum_xs.at[w, d - 1], sum_xr.at[w, d - 1], across_x[d - 1],
        )

    def sum_z(w, d):
        return remote(
            z_part.at[w, (z + d) % ZS], z_in.at[w, d - 1],
            sum_zs.at[w, d - 1], sum_zr.at[w, d - 1], across_z[d - 1],
        )

    def fin_z(w, d):
        return remote(
            z_done.at[w, z], z_done.at[w, z],
            fin_zs.at[w, d - 1], fin_zr.at[w, d - 1], across_z[d - 1],
        )

    def fin_x(w, d):
        return remote(
            x_done.at[w, x], x_done.at[w, x],
            fin_xs.at[w, d - 1], fin_xr.at[w, d - 1], across_x[d - 1],
        )

    def got_fin(ref, w, d, place, recv, device):
        remote(ref.at[w, place], ref.at[w, place], recv.at[w, d - 1], recv.at[w, d - 1], device).wait_recv()

    def scatter_x(w, total):
        x_part[w] = total.astype(BF16).reshape(XS, ROWS // XS, WIDTH)
        wg_acc[w] = total
        for d in range(1, XS):
            sum_x(w, d).start()

    def scatter_z(w):
        for d in range(1, XS):
            sum_x(w, d).wait_recv()
        total = wg_acc[w, pl.ds(x * (ROWS // XS), ROWS // XS)]
        for d in range(1, XS):
            total = total + x_in[w, d - 1].astype(F32)
        for q in range(ZS):
            part = total[16 * (q // 2) : 16 * (q // 2) + 16, 128 * (q % 2) : 128 * (q % 2) + 128]
            z_own[q] = part
            z_part[w, q] = part.astype(BF16)
        for d in range(1, ZS):
            sum_z(w, d).start()

    def gather_z(w):
        for d in range(1, ZS):
            sum_z(w, d).wait_recv()
        total = z_own[z]
        for d in range(1, ZS):
            total = total + z_in[w, d - 1].astype(F32)
        z_done[w, z] = total.astype(BF16)
        for d in range(1, ZS):
            fin_z(w, d).start()

    def gather_x(w):
        for d in range(1, ZS):
            got_fin(z_done, w, d, (z + ZS - d) % ZS, fin_zr, z_up)
        for q in range(ZS):
            x_done[w, x, 16 * (q // 2) : 16 * (q // 2) + 16, 128 * (q % 2) : 128 * (q % 2) + 128] = z_done[w, q]
        for d in range(1, XS):
            fin_x(w, d).start()

    def finish_sum(w):
        for d in range(1, XS):
            got_fin(x_done, w, d, (x + XS - d) % XS, fin_xr, x_up)
        for q in range(XS):
            wg_out[0, w, q * (ROWS // XS) : (q + 1) * (ROWS // XS)] = x_done[w, q].astype(F32)
        for d in range(1, XS):
            sum_x(w, d).wait_send()
            fin_x(w, d).wait_send()
        for d in range(1, ZS):
            sum_z(w, d).wait_send()
            fin_z(w, d).wait_send()

    def step(i, carry):
        t = i // 2
        layer = 1 - i % 2
        beta = beta_of(layer)

        @pl.when(i == 0)
        def _():
            grad_buf[...] = grad_in[0]

        @pl.when(i == 2)
        def _():
            remote(grad_buf, handed, hand_send, hand_recv, s_dn).wait()
            last = jnp.full((8, 128), section, I32)[0:1, 0:1] == SECTIONS - 1
            grad_buf[...] = jnp.where(
                last, grad_last[...].astype(F32), handed[...].astype(F32)
            ).astype(BF16)

        live = preact[0, t, layer].astype(F32) > 0
        masked32 = jnp.where(live, grad_buf[...].astype(F32), 0.0)
        masked = masked32.astype(BF16)
        masked_buf[...] = masked
        turned = lax.dot_general(
            masked, weights[0, layer], (((1,), (1,)), ((), ())), preferred_element_type=F32
        )
        image = ((1.0 - beta) * masked32 + beta * turned).astype(BF16)
        full[i, 0, 0] = image

        @pl.when(i == 0)
        def _():
            pl.semaphore_wait(barrier, len(peers))

        for h in range(2):
            send_side(i, h).start()
            send_up(i, 0, 0, h).start()
            send_dn(i, 0, 0, h).start()

        @pl.when(i == 0)
        def _():
            find_needs()
            for copy in need_copies:
                copy.start()

        @pl.when(i < 2)
        def _():
            build_dense(i)

        @pl.when(i == 0)
        def _():
            for copy in need_copies:
                copy.wait()

        def relay(c, m, h):
            up, dn = 8 - m, m
            if m < 4 or h == 0:
                got_full(i, c, up, h)
                if m < 3 or (m == 3 and h == 0):
                    send_up(i, c, up, h).start()
            if m < 4 or h == 1:
                got_full(i, c, dn, h)
                if m < 3 or (m == 3 and h == 1):
                    send_dn(i, c, dn, h).start()

        def pass_on(c, k):
            table = need_m if c == 0 else need_p
            line = table[pl.ds(t * 16 + c * 8 + k, 1), :].astype(BF16)
            second = jnp.concatenate([line, line], axis=1)
            first = 1.0 - second
            pick[c, k] = full[i, c, k, tile(0)] * first + full[i, c, k, tile(1)] * second
            send_pick(i, c, k).start()

        def product(j):
            block = full[i, j // 8, j % 8] if j < 16 else half[i, j - 16]
            return jnp.dot(dense[t, j], block, preferred_element_type=F32)

        def add_products(chunks):
            acc[...] += sum(product(j) for j in chunks)

        for h in range(2):
            got_full(i, 1, 0, h)
            send_up(i, 1, 0, h).start()
            send_dn(i, 1, 0, h).start()
        pass_on(0, 0)
        pass_on(1, 0)
        shown = ALPHA * full[i, 0, 0].astype(F32)
        term = beta * lax.dot_general(
            support[0, t, layer], masked_buf[...], (((0,), (0,)), ((), ())),
            preferred_element_type=F32,
        )

        @pl.when(layer == 1)
        def _():
            init_out[0, t] = shown

        @pl.when(layer == 0)
        def _():
            init_out[0, t] += shown

        @pl.when(t == 0)
        def _():
            wg_acc[layer] = term

        @pl.when(t == 1)
        def _():
            scatter_x(layer, wg_acc[layer] + term)

        acc[...] = product(0) + product(8)

        for m in range(1, 5):
            ks = (8 - m, m) if m < 4 else (4,)
            for c in range(2):
                for h in range(2):
                    relay(c, m, h)
                for k in ks:
                    pass_on(c, k)
                add_products([8 * c + k for k in ks])
            before = (9 - m, m - 1) if m > 1 else (0,)
            for k in before:
                got_half(i, 0, k)
                got_half(i, 1, k)
            add_products([16 + k for k in before])

            @pl.when(t == 1)
            def _():
                if m == 1:
                    scatter_z(layer)
                elif m == 2:
                    gather_z(layer)
                elif m == 3:
                    gather_x(layer)

        for c in range(2):
            got_half(i, c, 4)
        grad = ((1.0 - ALPHA) * (acc[...] + product(20))).astype(BF16)
        grad_buf[...] = grad

        @pl.when(layer == 0)
        def _():
            hand_out[t, 0] = grad

        @pl.when(i == 1)
        def _():
            remote(grad_buf, handed, hand_send, hand_recv, s_dn).start()

        @pl.when(t == 1)
        def _():
            finish_sum(layer)

        for copy in all_sends(i):
            copy.wait_send()
        return carry

    lax.fori_loop(0, 4, step, 0)


def write_results(*refs):
    sources, targets, staged, (in_sem, out_sem) = refs[:3], refs[3:6], refs[6:9], refs[9:]
    come = [pltpu.make_async_copy(a, b, in_sem.at[n]) for n, (a, b) in enumerate(zip(sources, staged))]
    go = [pltpu.make_async_copy(a, b, out_sem.at[n]) for n, (a, b) in enumerate(zip(staged, targets))]
    for copy in come:
        copy.start()
    for first, second in zip(come, go):
        first.wait()
        second.start()
    for copy in go:
        copy.wait()


def shards(grad_in, grad_last, support, preact, weights, tile_vals, tile_row, tile_col, tile_count):
    vmem = pl.BlockSpec(memory_space=pltpu.VMEM)
    shapes = (
        jax.ShapeDtypeStruct((2, 1, ROWS, WIDTH), BF16),
        jax.ShapeDtypeStruct((1, 2, ROWS, WIDTH), F32),
        jax.ShapeDtypeStruct((1, 2, WIDTH, WIDTH), F32),
    )
    results = pl.pallas_call(
        kernel,
        out_shape=shapes,
        in_specs=[vmem] * 5
        + [pl.BlockSpec(memory_space=pl.ANY), vmem, vmem, vmem],
        out_specs=(vmem, vmem, vmem),
        scratch_shapes=[
            pltpu.VMEM((2, WIDTH, WIDTH), F32),
            pltpu.VMEM((2, XS, ROWS // XS, WIDTH), BF16),
            pltpu.VMEM((2, XS - 1, ROWS // XS, WIDTH), BF16),
            pltpu.VMEM((ZS, 16, 128), F32),
            pltpu.VMEM((2, ZS, 16, 128), BF16),
            pltpu.VMEM((2, ZS - 1, 16, 128), BF16),
            pltpu.VMEM((2, ZS, 16, 128), BF16),
            pltpu.VMEM((2, XS, ROWS // XS, WIDTH), BF16),
            pltpu.VMEM((2, LIST, TILE, TILE), BF16),
            pltpu.VMEM((8, 128), I32),
            pltpu.VMEM((8, 128), I32),
            pltpu.SMEM((8, 128), I32),
            pltpu.VMEM((32, 128), F32),
            pltpu.VMEM((32, 128), F32),
            pltpu.VMEM((32, 128), F32),
            pltpu.VMEM((LIST, TILE, TILE), F32),
            pltpu.VMEM((2, CHUNKS, 256, 256), BF16),
            pltpu.VMEM((4, 2, ZS, ROWS, WIDTH), BF16),
            pltpu.VMEM((4, ZS, 2 * TILE, WIDTH), BF16),
            pltpu.VMEM((2, ZS, TILE, WIDTH), BF16),
            pltpu.VMEM((ROWS, WIDTH), BF16),
            pltpu.VMEM((ROWS, WIDTH), BF16),
            pltpu.VMEM((ROWS, WIDTH), F32),
            pltpu.VMEM((ROWS, WIDTH), BF16),
            pltpu.SemaphoreType.DMA((2,)),
            pltpu.SemaphoreType.DMA,
            pltpu.SemaphoreType.DMA((2,)),
            pltpu.SemaphoreType.DMA((2,)),
            pltpu.SemaphoreType.DMA((3, 2, ZS, 2)),
            pltpu.SemaphoreType.DMA((4, 2, ZS, 2)),
            pltpu.SemaphoreType.DMA((2, ZS)),
            pltpu.SemaphoreType.DMA((4, 2, ZS)),
            pltpu.SemaphoreType.DMA,
            pltpu.SemaphoreType.DMA,
        ]
        + [pltpu.SemaphoreType.DMA((2, n - 1)) for n in (XS, XS, ZS, ZS, ZS, ZS, XS, XS)],
        compiler_params=pltpu.CompilerParams(
            collective_id=0, has_side_effects=True, vmem_limit_bytes=60 * 1024 * 1024
        ),
    )(grad_in, grad_last, support, preact, weights, tile_vals, tile_row, tile_col, tile_count)
    anywhere = pl.BlockSpec(memory_space=pl.ANY)
    return pl.pallas_call(
        write_results,
        out_shape=shapes,
        in_specs=[anywhere] * 3,
        out_specs=(anywhere,) * 3,
        scratch_shapes=[pltpu.VMEM(s.shape, s.dtype) for s in shapes]
        + [pltpu.SemaphoreType.DMA((3,)), pltpu.SemaphoreType.DMA((3,))],
    )(*results)


def solution(mesh):
    return jax.shard_map(
        shards,
        mesh=mesh,
        in_specs=(
            P("section", "rows", None),
            P("rows", None),
            P("section", None, None, "rows", None),
            P("section", None, None, "rows", None),
            P("section", None, None, None),
            P("section", None, "rows", None, None),
            P("section", None, "rows"),
            P("section", None, "rows"),
            P("section", None, "rows"),
        ),
        out_specs=(
            P(None, "section", "rows", None),
            P("section", None, "rows", None),
            P("section", None, None, None),
        ),
        check_vma=False,
    )
```

```python
import jax
import jax.numpy as jnp
from jax import lax
from jax.experimental import pallas as pl
from jax.experimental.pallas import tpu as pltpu
from jax.sharding import PartitionSpec as P

ALPHA = 0.1
BETA_SCALE = 0.5
MESH = pl.DeviceIdType.MESH

SECTIONS = 8
XS = 4
ZS = 8
TILE = 128
WIDTH = 256
ROWS = 256
LIST = 96
RA = 64
RC = TILE - RA
ARRIVALS = (
    (1, 0, 0), (1, 0, 1), (0, 7, 0), (0, 1, 0), (0, 7, 1), (0, 1, 1), (1, 7, 0), (1, 1, 0), (1, 7, 1), (1, 1, 1),
    (0,),
    (0, 6, 0), (0, 2, 0), (0, 6, 1), (0, 2, 1), (1, 6, 0), (1, 2, 0), (1, 6, 1), (1, 2, 1),
    (7,), (0, 5, 0), (0, 3, 0), (1,),
    (0, 5, 1), (0, 3, 1), (1, 5, 0), (1, 3, 0), (1, 5, 1), (1, 3, 1),
    (6,), (0, 4, 0), (2,), (1, 4, 0), (0, 4, 1), (1, 4, 1), (5,), (3,), (4,),
)
F32 = jnp.float32
BF16 = jnp.bfloat16
I32 = jnp.int32


def kernel(
    grad_in, grad_last, support, preact, weights, vals_hbm, row_in, col_in, count_in,
    hand_out, init_out, wg_out,
    wg_acc, x_part, x_in, z_own, z_part, z_in, z_done, x_done,
    vals, key_buf, tab_v, tab_s, need, need_at, run, near_adj, far_adj,
    full, side, far, pick1, pick2a, pick3, pick2c, grad_buf, masked_buf, acc, handed,
    vals_sem, tab_sem, need_send, need_recv, full_up, full_dn, full_recv,
    side_first, side_up, side_dn, side_recv, far_send, far_recv,
    hand_send, hand_recv, sum_xs, sum_xr, sum_zs, sum_zr, fin_zs, fin_zr, fin_xs, fin_xr,
):
    section = lax.axis_index("section")
    me = lax.axis_index("rows")
    x = me // ZS
    z = me % ZS

    def at(sec, xx, zz):
        return (sec, xx * ZS + zz)

    across_x = [at(section, (x + d) % XS, z) for d in range(1, XS)]
    across_z = [at(section, x, (z + d) % ZS) for d in range(1, ZS)]
    x_up, x_far, x_dn = across_x
    z_up, z_dn = across_z[0], across_z[-1]
    s_up = at((section + 1) % SECTIONS, x, z)
    s_dn = at((section + SECTIONS - 1) % SECTIONS, x, z)

    for t in range(2):
        pltpu.make_async_copy(vals_hbm.at[0, t], vals.at[t], vals_sem.at[t]).start()

    barrier = pltpu.get_barrier_semaphore()
    peers = across_x + across_z + [s_up, s_dn]
    for peer in peers:
        pl.semaphore_signal(barrier, inc=1, device_id=peer, device_id_type=MESH)

    def remote(src, dst, send, recv, device):
        return pltpu.make_async_remote_copy(
            src_ref=src, dst_ref=dst, send_sem=send, recv_sem=recv,
            device_id=device, device_id_type=MESH,
        )

    def tile(h):
        return pl.ds(h * TILE, TILE)

    def late(h):
        return pl.ds(h * RC, RC)

    def send_full(i, k, h, up):
        k_to = (k + (7 if up else 1)) % ZS
        return remote(
            full.at[i, k, tile(h)], full.at[i, k_to, tile(h)],
            (full_up if up else full_dn).at[k, h], full_recv.at[i, k_to, h], z_up if up else z_dn,
        )

    def send_side(i, k, h, up):
        k_to = (k + (7 if up else 1)) % ZS
        return remote(
            side.at[i, k, late(h)], side.at[i, k_to, late(h)],
            (side_up if up else side_dn).at[k, h], side_recv.at[i, k_to, h], z_up if up else z_dn,
        )

    def first_side(i, h):
        return remote(
            full.at[i, 0, pl.ds(h * TILE + RA, RC)], side.at[i, 0, late(h)],
            side_first.at[h], side_recv.at[i, 0, h], x_up,
        )

    def send_far(i, k, n):
        source, start, size, device = (
            (pick1.at[k], 0, TILE, x_dn),
            (pick2a.at[k], TILE, RA, x_far),
            (pick3.at[k], 2 * TILE, RA, x_up),
            (pick2c.at[k], TILE + RA, RC, x_up),
        )[n]
        return remote(
            source, far.at[i, k, pl.ds(start, size)], far_send.at[n, k], far_recv.at[i, n, k], device
        )

    def moves(c, k, h):
        up = k in (0, 7, 6) or (k == 5 and h == 0)
        dn = k in (0, 1, 2) or (k == 3 and h == 1)
        return [way for way, goes in ((True, up), (False, dn)) if goes]

    need_copies = [
        remote(need, need_at.at[n], need_send.at[n], need_recv.at[n], device)
        for n, device in enumerate((x_up, x_far, x_dn))
    ]

    def all_sends(i):
        copies = [first_side(i, h) for h in range(2)]
        for k in range(ZS):
            for h in range(2):
                for way in moves(0, k, h):
                    copies += [send_full(i, k, h, way), send_side(i, k, h, way)]
            copies += [send_far(i, k, n) for n in range(4)]
        return copies

    def beta_of(layer):
        depth = (2 * section + layer + 1).astype(F32)
        return jnp.log(BETA_SCALE / jnp.full((8, 128), depth, F32) + 1.0)[0:1, 0:1]

    def find_needs():
        slot = lax.broadcasted_iota(I32, (24, LIST), 0)
        owner = ((x + 1 + (slot >> 3)) & 3) * ZS + ((z + slot) & 7)
        for t in range(2):
            col = jnp.broadcast_to(col_in[0, t : t + 1, :], (24, LIST))
            second = jnp.where((col >> 1) == owner, (col & 1).astype(F32), 0.0)
            need[t * 24 : (t + 1) * 24, :] = jnp.broadcast_to(
                jnp.max(second, axis=1, keepdims=True), (24, 128)
            )

    def sort_entries(t):
        col = col_in[0, t : t + 1, :]
        owner = col >> 1
        dx = ((owner >> 3) - x) & 3
        dz = ((owner & 7) - z) & 7
        key = jnp.where(dx == 0, dz * 4 + (col & 1) * 2, 32 + dz * 6 + (dx - 1) * 2)
        key = key + row_in[0, t : t + 1, :]
        place = lax.broadcasted_iota(I32, (1, LIST), 1)
        key = jnp.where(place < count_in[0, :, t : t + 1], key, 127)
        key_buf[...] = jnp.full((8, 128), 127, I32)
        key_buf[0:1, 0:LIST] = key
        across = jnp.broadcast_to(key_buf[0:1, :], (128, 128))
        down = across.T
        lane = lax.broadcasted_iota(I32, (128, 128), 1)
        sub = lax.broadcasted_iota(I32, (128, 128), 0)

        def count(hit, axis):
            return jnp.sum(jnp.where(hit, 1, 0), axis=axis, keepdims=True)

        rank = count((across < down) | ((across == down) & (lane < sub)), 1)

        def pull(values, position):
            return jnp.sum(jnp.where(rank == position, values, 0), axis=0, keepdims=True)

        order = pull(sub, lane)
        same = jnp.where(
            (pull(down, lane) == pull(down, lane - 1)) & (lane[0:1, :] > 0), 1, 0
        )
        last = jnp.maximum(count(down <= lane, 0) - 1, 0)
        there = jnp.where(count(down == lane, 0) > 0, 1, 0)
        for r, line in enumerate((order, same, last, there)):
            tab_v[r : r + 1, :] = line
        fetch = pltpu.make_async_copy(tab_v, tab_s, tab_sem)
        fetch.start()
        fetch.wait()

    def build_adjacency(t):
        sort_entries(t)

        def add(e, total):
            total = total * tab_s[1, e].astype(F32) + vals[t, tab_s[0, e]].astype(F32)
            run[e] = total
            return total

        lax.fori_loop(0, LIST, add, jnp.zeros((TILE, TILE), F32), unroll=4)

        def summed(slot):
            return (run[tab_s[2, slot]] * tab_s[3, slot].astype(F32)).astype(BF16)

        def fill(k, carry):
            for r in range(2):
                for h in range(2):
                    near_adj[t, k, tile(r), tile(h)] = summed(k * 4 + h * 2 + r)
                for q in range(3):
                    far_adj[t, k, tile(r), tile(q)] = summed(32 + k * 6 + q * 2 + r)
            return carry

        lax.fori_loop(0, ZS, fill, 0)

    def sum_x(w, d):
        return remote(
            x_part.at[w, (x + d) % XS], x_in.at[w, d - 1],
            sum_xs.at[w, d - 1], sum_xr.at[w, d - 1], across_x[d - 1],
        )

    def sum_z(w, d):
        return remote(
            z_part.at[w, (z + d) % ZS], z_in.at[w, d - 1],
            sum_zs.at[w, d - 1], sum_zr.at[w, d - 1], across_z[d - 1],
        )

    def fin_z(w, d):
        return remote(
            z_done.at[w, z], z_done.at[w, z],
            fin_zs.at[w, d - 1], fin_zr.at[w, d - 1], across_z[d - 1],
        )

    def fin_x(w, d):
        return remote(
            x_done.at[w, x], x_done.at[w, x],
            fin_xs.at[w, d - 1], fin_xr.at[w, d - 1], across_x[d - 1],
        )

    def got_fin(ref, w, d, place, recv, device):
        remote(ref.at[w, place], ref.at[w, place], recv.at[w, d - 1], recv.at[w, d - 1], device).wait_recv()

    def scatter_x(w, total):
        x_part[w] = total.astype(BF16).reshape(XS, ROWS // XS, WIDTH)
        wg_acc[w] = total
        for d in range(1, XS):
            sum_x(w, d).start()

    def scatter_z(w):
        for d in range(1, XS):
            sum_x(w, d).wait_recv()
        total = wg_acc[w, pl.ds(x * (ROWS // XS), ROWS // XS)]
        for d in range(1, XS):
            total = total + x_in[w, d - 1].astype(F32)
        for q in range(ZS):
            part = total[16 * (q // 2) : 16 * (q // 2) + 16, 128 * (q % 2) : 128 * (q % 2) + 128]
            z_own[q] = part
            z_part[w, q] = part.astype(BF16)
        for d in range(1, ZS):
            sum_z(w, d).start()

    def gather_z(w):
        for d in range(1, ZS):
            sum_z(w, d).wait_recv()
        total = z_own[z]
        for d in range(1, ZS):
            total = total + z_in[w, d - 1].astype(F32)
        z_done[w, z] = total.astype(BF16)
        for d in range(1, ZS):
            fin_z(w, d).start()

    def gather_x(w):
        for d in range(1, ZS):
            got_fin(z_done, w, d, (z + ZS - d) % ZS, fin_zr, z_up)
        for q in range(ZS):
            x_done[w, x, 16 * (q // 2) : 16 * (q // 2) + 16, 128 * (q % 2) : 128 * (q % 2) + 128] = z_done[w, q]
        for d in range(1, XS):
            fin_x(w, d).start()

    def finish_sum(w):
        for d in range(1, XS):
            got_fin(x_done, w, d, (x + XS - d) % XS, fin_xr, x_up)
        for q in range(XS):
            wg_out[0, w, q * (ROWS // XS) : (q + 1) * (ROWS // XS)] = x_done[w, q].astype(F32)
        for d in range(1, XS):
            sum_x(w, d).wait_send()
            fin_x(w, d).wait_send()
        for d in range(1, ZS):
            sum_z(w, d).wait_send()
            fin_z(w, d).wait_send()

    find_needs()

    def step(i, carry):
        t = i // 2
        layer = 1 - i % 2
        beta = beta_of(layer)

        @pl.when(i == 0)
        def _():
            grad_buf[...] = grad_in[0]
            pl.semaphore_wait(barrier, len(peers))
            for copy in need_copies:
                copy.start()

        @pl.when(i == 2)
        def _():
            remote(grad_buf, handed, hand_send, hand_recv, s_dn).wait()
            last = jnp.full((8, 128), section, I32)[0:1, 0:1] == SECTIONS - 1
            grad_buf[...] = jnp.where(
                last, grad_last[...].astype(F32), handed[...].astype(F32)
            ).astype(BF16)

        for h in range(2):
            live = preact[0, t, layer, tile(h)].astype(F32) > 0
            masked32 = jnp.where(live, grad_buf[tile(h)].astype(F32), 0.0)
            masked = masked32.astype(BF16)
            masked_buf[tile(h)] = masked
            turned = lax.dot_general(
                masked, weights[0, layer], (((1,), (1,)), ((), ())), preferred_element_type=F32
            )
            full[i, 0, tile(h)] = ((1.0 - beta) * masked32 + beta * turned).astype(BF16)
            first_side(i, h).start()
            for way in (True, False):
                send_full(i, 0, h, way).start()

        shown = ALPHA * full[i, 0].astype(F32)
        term = beta * lax.dot_general(
            support[0, t, layer], masked_buf[...], (((0,), (0,)), ((), ())),
            preferred_element_type=F32,
        )

        @pl.when(t == 0)
        def _():
            wg_acc[layer] = term

        @pl.when(t == 1)
        def _():
            scatter_x(layer, wg_acc[layer] + term)

        @pl.when(layer == 1)
        def _():
            init_out[0, t] = shown

        @pl.when(layer == 0)
        def _():
            init_out[0, t] += shown

        @pl.when(i == 0)
        def _():
            for u in range(2):
                pltpu.make_async_copy(vals_hbm.at[0, u], vals.at[u], vals_sem.at[u]).wait()
            build_adjacency(0)
            for copy in need_copies:
                copy.wait()

        def chosen(table, q, k):
            line = table[pl.ds(t * 24 + (q - 1) * 8 + k, 1), :].astype(BF16)
            second = jnp.concatenate([line, line], axis=1)
            return 1.0 - second, second

        from_dn, from_far, from_up = (need_at.at[n] for n in range(3))

        def pass_full(k):
            for table, q, n, target, rows in (
                (from_dn, 1, 0, pick1, TILE), (from_far, 2, 1, pick2a, RA), (from_up, 3, 2, pick3, RA)
            ):
                first, second = chosen(table, q, k)
                target[k] = (
                    full[i, k, 0:rows] * first + full[i, k, TILE : TILE + rows] * second
                )
                send_far(i, k, n).start()

        def pass_side(k):
            first, second = chosen(from_up, 2, k)
            pick2c[k] = side[i, k, 0:RC] * first + side[i, k, RC : 2 * RC] * second
            send_far(i, k, 3).start()
            first, second = chosen(need, 3, k)
            far[i, k, 2 * TILE + RA : 3 * TILE] = (
                side[i, k, 0:RC] * first + side[i, k, RC : 2 * RC] * second
            )

        def product(k, near):
            adjacency, block = (near_adj[t, k], full[i, k]) if near else (far_adj[t, k], far[i, k])
            return jnp.dot(adjacency, block, preferred_element_type=F32)

        pass_full(0)

        @pl.when(i == 1)
        def _():
            build_adjacency(1)

        acc[...] = product(0, True)

        for n, arrival in enumerate(ARRIVALS):
            if len(arrival) == 1:
                (k,) = arrival
                for part in range(4):
                    send_far(i, k, part).wait_recv()
                if k != 4:
                    acc[...] += product(k, False)
            else:
                c, k, h = arrival
                if c == 0:
                    remote(
                        full.at[i, k, tile(h)], full.at[i, k, tile(h)],
                        full_up.at[k, h], full_recv.at[i, k, h], z_up,
                    ).wait_recv()
                else:
                    remote(
                        side.at[i, k, late(h)], side.at[i, k, late(h)],
                        side_up.at[k, h], side_recv.at[i, k, h], z_up,
                    ).wait_recv()
                for way in moves(c, k, h):
                    (send_side if c else send_full)(i, k, h, way).start()
                if h == 1:
                    if c:
                        pass_side(k)
                    else:
                        pass_full(k)
                        acc[...] += product(k, True)

            @pl.when(t == 1)
            def _():
                if arrival == (0,):
                    scatter_z(layer)
                elif arrival == (7,):
                    gather_z(layer)
                elif arrival == (6,):
                    gather_x(layer)

        grad = ((1.0 - ALPHA) * (acc[...] + product(4, False))).astype(BF16)
        grad_buf[...] = grad

        @pl.when(i == 1)
        def _():
            remote(grad_buf, handed, hand_send, hand_recv, s_dn).start()

        @pl.when(layer == 0)
        def _():
            hand_out[t, 0] = grad

        @pl.when(t == 1)
        def _():
            finish_sum(layer)

        for copy in all_sends(i):
            copy.wait_send()
        return carry

    lax.fori_loop(0, 4, step, 0)


def write_results(*refs):
    sources, targets, staged, (in_sem, out_sem) = refs[:3], refs[3:6], refs[6:9], refs[9:]
    come = [pltpu.make_async_copy(a, b, in_sem.at[n]) for n, (a, b) in enumerate(zip(sources, staged))]
    go = [pltpu.make_async_copy(a, b, out_sem.at[n]) for n, (a, b) in enumerate(zip(staged, targets))]
    for copy in come:
        copy.start()
    for first, second in zip(come, go):
        first.wait()
        second.start()
    for copy in go:
        copy.wait()


def shards(grad_in, grad_last, support, preact, weights, tile_vals, tile_row, tile_col, tile_count):
    vmem = pl.BlockSpec(memory_space=pltpu.VMEM)
    shapes = (
        jax.ShapeDtypeStruct((2, 1, ROWS, WIDTH), BF16),
        jax.ShapeDtypeStruct((1, 2, ROWS, WIDTH), F32),
        jax.ShapeDtypeStruct((1, 2, WIDTH, WIDTH), F32),
    )
    results = pl.pallas_call(
        kernel,
        out_shape=shapes,
        in_specs=[vmem] * 5
        + [pl.BlockSpec(memory_space=pl.ANY), vmem, vmem, vmem],
        out_specs=(vmem, vmem, vmem),
        scratch_shapes=[
            pltpu.VMEM((2, WIDTH, WIDTH), F32),
            pltpu.VMEM((2, XS, ROWS // XS, WIDTH), BF16),
            pltpu.VMEM((2, XS - 1, ROWS // XS, WIDTH), BF16),
            pltpu.VMEM((ZS, 16, 128), F32),
            pltpu.VMEM((2, ZS, 16, 128), BF16),
            pltpu.VMEM((2, ZS - 1, 16, 128), BF16),
            pltpu.VMEM((2, ZS, 16, 128), BF16),
            pltpu.VMEM((2, XS, ROWS // XS, WIDTH), BF16),
            pltpu.VMEM((2, LIST, TILE, TILE), BF16),
            pltpu.VMEM((8, 128), I32),
            pltpu.VMEM((8, 128), I32),
            pltpu.SMEM((8, 128), I32),
            pltpu.VMEM((48, 128), F32),
            pltpu.VMEM((3, 48, 128), F32),
            pltpu.VMEM((LIST, TILE, TILE), F32),
            pltpu.VMEM((2, ZS, ROWS, 2 * TILE), BF16),
            pltpu.VMEM((2, ZS, ROWS, 3 * TILE), BF16),
            pltpu.VMEM((4, ZS, ROWS, WIDTH), BF16),
            pltpu.VMEM((4, ZS, 2 * RC, WIDTH), BF16),
            pltpu.VMEM((4, ZS, 3 * TILE, WIDTH), BF16),
            pltpu.VMEM((ZS, TILE, WIDTH), BF16),
            pltpu.VMEM((ZS, RA, WIDTH), BF16),
            pltpu.VMEM((ZS, RA, WIDTH), BF16),
            pltpu.VMEM((ZS, RC, WIDTH), BF16),
            pltpu.VMEM((ROWS, WIDTH), BF16),
            pltpu.VMEM((ROWS, WIDTH), BF16),
            pltpu.VMEM((ROWS, WIDTH), F32),
            pltpu.VMEM((ROWS, WIDTH), BF16),
            pltpu.SemaphoreType.DMA((2,)),
            pltpu.SemaphoreType.DMA,
            pltpu.SemaphoreType.DMA((3,)),
            pltpu.SemaphoreType.DMA((3,)),
            pltpu.SemaphoreType.DMA((ZS, 2)),
            pltpu.SemaphoreType.DMA((ZS, 2)),
            pltpu.SemaphoreType.DMA((4, ZS, 2)),
            pltpu.SemaphoreType.DMA((2,)),
            pltpu.SemaphoreType.DMA((ZS, 2)),
            pltpu.SemaphoreType.DMA((ZS, 2)),
            pltpu.SemaphoreType.DMA((4, ZS, 2)),
            pltpu.SemaphoreType.DMA((4, ZS)),
            pltpu.SemaphoreType.DMA((4, 4, ZS)),
            pltpu.SemaphoreType.DMA,
            pltpu.SemaphoreType.DMA,
        ]
        + [pltpu.SemaphoreType.DMA((2, n - 1)) for n in (XS, XS, ZS, ZS, ZS, ZS, XS, XS)],
        compiler_params=pltpu.CompilerParams(
            collective_id=0, has_side_effects=True, vmem_limit_bytes=60 * 1024 * 1024
        ),
    )(grad_in, grad_last, support, preact, weights, tile_vals, tile_row, tile_col, jnp.swapaxes(tile_count, 1, 2))
    anywhere = pl.BlockSpec(memory_space=pl.ANY)
    return pl.pallas_call(
        write_results,
        out_shape=shapes,
        in_specs=[anywhere] * 3,
        out_specs=(anywhere,) * 3,
        scratch_shapes=[pltpu.VMEM(s.shape, s.dtype) for s in shapes]
        + [pltpu.SemaphoreType.DMA((3,)), pltpu.SemaphoreType.DMA((3,))],
    )(*results)


def solution(mesh):
    return jax.shard_map(
        shards,
        mesh=mesh,
        in_specs=(
            P("section", "rows", None),
            P("rows", None),
            P("section", None, None, "rows", None),
            P("section", None, None, "rows", None),
            P("section", None, None, None),
            P("section", None, "rows", None, None),
            P("section", None, "rows"),
            P("section", None, "rows"),
            P("section", None, "rows"),
        ),
        out_specs=(
            P(None, "section", "rows", None),
            P("section", None, "rows", None),
            P("section", None, None, None),
        ),
        check_vma=False,
    )
```

```python
import jax
import jax.numpy as jnp
from jax import lax
from jax.experimental import pallas as pl
from jax.experimental.pallas import tpu as pltpu
from jax.sharding import PartitionSpec as P

ALPHA = 0.1
BETA_SCALE = 0.5
MESH = pl.DeviceIdType.MESH

SECTIONS = 8
XS = 4
ZS = 8
TILE = 128
WIDTH = 256
ROWS = 256
LIST = 96
RA = 80
PIECES = 4
RC = TILE - RA
PHASES = (16, 39, 48)
ARRIVALS = (
    (1, 0, 0), (0, 7, 0), (0, 1, 0), (1, 0, 1), (0, 7, 1), (0, 1, 1), (0, 7, 2), (0, 1, 2), (0, 7, 3), (0, 1, 3),
    (1, 7, 0), (1, 1, 0), (0, 6, 0), (0, 2, 0), (0,), (1, 7, 1), (1, 1, 1), (0, 6, 1), (0, 2, 1), (0, 6, 2),
    (0, 2, 2), (0, 6, 3), (0, 2, 3), (1, 6, 0), (1, 2, 0), (0, 5, 0), (0, 3, 0), (1, 6, 1), (1, 2, 1), (0, 5, 1),
    (0, 3, 1), (7,), (0, 5, 2), (1,), (0, 3, 2), (0, 5, 3), (0, 3, 3), (1, 5, 0), (1, 3, 0), (0, 4, 0), (1, 3, 1),
    (1, 5, 1), (0, 4, 1), (0, 4, 2), (6,), (2,), (0, 4, 3), (1, 4, 0), (1, 4, 1), (5,), (3,), (4,),
)
F32 = jnp.float32
BF16 = jnp.bfloat16
I32 = jnp.int32


def kernel(
    grad_hbm, last_hbm, support_hbm, preact_hbm, weights_hbm, vals_hbm, row_hbm, col_hbm, count_hbm,
    hand_hbm, init_hbm, wg_hbm,
    hand_out, init_out, wg_out,
    row_in, col_in, count_in, grad_last, support, preact, weights, preact_dn, weights_dn, masked_dn, image_dn,
    masked_in, wg_acc, x_part, x_in, z_own, z_part, z_in, done,
    vals, key_buf, tab_v, tab_s, need, need_at, run, near_adj, far_adj,
    full, side, far, pick1, pick2a, pick3, pick2c, grad_buf, masked_buf, acc,
    in_sem, out_sem, vals_sem, tab_sem, need_send, need_recv, full_up, full_dn, full_recv,
    side_first, side_up, side_dn, side_recv, far_send, far_recv,
    lend_send, lend_recv, own_send, own_recv, mask_send, mask_recv, next_up, next_dn, next_side, sum_xs, sum_xr, sum_zs, sum_zr, fin_zs, fin_zr, fin_xs, fin_xr,
):
    section = lax.axis_index("section")
    me = lax.axis_index("rows")
    x = me // ZS
    z = me % ZS

    def at(sec, xx, zz):
        return (sec, xx * ZS + zz)

    across_x = [at(section, (x + d) % XS, z) for d in range(1, XS)]
    across_z = [at(section, x, (z + d) % ZS) for d in range(1, ZS)]
    x_up, x_far, x_dn = across_x
    z_up, z_dn = across_z[0], across_z[-1]
    above, below = (section + 1) % SECTIONS, (section + SECTIONS - 1) % SECTIONS
    s_up, s_dn = at(above, x, z), at(below, x, z)
    dn_side = at(below, (x + 1) % XS, z)
    dn_z_up, dn_z_dn = at(below, x, (z + 1) % ZS), at(below, x, (z + ZS - 1) % ZS)
    up_peers = [at(above, (x + XS - 1) % XS, z), at(above, x, (z + ZS - 1) % ZS), at(above, x, (z + 1) % ZS)]

    barrier = pltpu.get_barrier_semaphore()
    peers = across_x + across_z + [s_up, s_dn, dn_side, dn_z_up, dn_z_dn] + up_peers
    for peer in peers:
        pl.semaphore_signal(barrier, inc=1, device_id=peer, device_id_type=MESH)

    inputs = [
        pltpu.make_async_copy(source, target, in_sem.at[n])
        for n, (source, target) in enumerate((
            (grad_hbm.at[0], grad_buf),
            (preact_hbm.at[0], preact),
            (weights_hbm.at[0], weights),
            (col_hbm, col_in),
            (row_hbm, row_in),
            (count_hbm, count_in),
            (support_hbm.at[0], support),
            (last_hbm, grad_last),
        ))
    ] + [pltpu.make_async_copy(vals_hbm.at[0, t], vals.at[t], vals_sem.at[t]) for t in range(2)]
    for copy in inputs:
        copy.start()

    def remote(src, dst, send, recv, device):
        return pltpu.make_async_remote_copy(
            src_ref=src, dst_ref=dst, send_sem=send, recv_sem=recv,
            device_id=device, device_id_type=MESH,
        )

    def tile(h):
        return pl.ds(h * TILE, TILE)

    def piece(p):
        return pl.ds(p * (ROWS // PIECES), ROWS // PIECES)

    def late(h):
        return pl.ds(h * RC, RC)

    def send_full(i, k, h, up):
        k_to = (k + (7 if up else 1)) % ZS
        return remote(
            full.at[i, k, piece(h)], full.at[i, k_to, piece(h)],
            (full_up if up else full_dn).at[k, h], full_recv.at[i, k_to, h], z_up if up else z_dn,
        )

    def send_side(i, k, h, up):
        k_to = (k + (7 if up else 1)) % ZS
        return remote(
            side.at[i, k, late(h)], side.at[i, k_to, late(h)],
            (side_up if up else side_dn).at[k, h], side_recv.at[i, k_to, h], z_up if up else z_dn,
        )

    def first_side(i, h):
        return remote(
            full.at[i, 0, pl.ds(h * TILE + RA, RC)], side.at[i, 0, late(h)],
            side_first.at[h], side_recv.at[i, 0, h], x_up,
        )

    def send_far(i, k, n):
        source, start, size, device = (
            (pick1.at[k], 0, TILE, x_dn),
            (pick2a.at[k], TILE, RA, x_far),
            (pick3.at[k], 2 * TILE, RA, x_up),
            (pick2c.at[k], TILE + RA, RC, x_up),
        )[n]
        return remote(
            source, far.at[i, k, pl.ds(start, size)], far_send.at[n, k], far_recv.at[i, n, k], device
        )

    def moves(c, k, h):
        first = h < (1 if c else PIECES // 2)
        up = k in (0, 7, 6) or (k == 5 and first)
        dn = k in (0, 1, 2) or (k == 3 and not first)
        return [way for way, goes in ((True, up), (False, dn)) if goes]

    need_copies = [
        remote(need, need_at.at[n], need_send.at[n], need_recv.at[n], device)
        for n, device in enumerate((x_up, x_far, x_dn))
    ]

    def all_sends(i):
        copies = []
        for k in range(ZS):
            if k:
                copies += [send_full(i, k, p, way) for p in range(PIECES) for way in moves(0, k, p)]
            copies += [send_side(i, k, h, way) for h in range(2) for way in moves(1, k, h)]
            copies += [send_far(i, k, n) for n in range(4)]
        return copies

    def beta_of(place, layer):
        depth = (2 * place + layer + 1).astype(F32)
        return jnp.log(BETA_SCALE / jnp.full((8, 128), depth, F32) + 1.0)[0:1, 0:1]

    def find_needs():
        slot = lax.broadcasted_iota(I32, (24, LIST), 0)
        owner = ((x + 1 + (slot >> 3)) & 3) * ZS + ((z + slot) & 7)
        for t in range(2):
            col = jnp.broadcast_to(col_in[0, t : t + 1, :], (24, LIST))
            second = jnp.where((col >> 1) == owner, (col & 1).astype(F32), 0.0)
            need[t * 24 : (t + 1) * 24, :] = jnp.broadcast_to(
                jnp.max(second, axis=1, keepdims=True), (24, 128)
            )

    def sort_entries(t):
        col = col_in[0, t : t + 1, :]
        owner = col >> 1
        dx = ((owner >> 3) - x) & 3
        dz = ((owner & 7) - z) & 7
        key = jnp.where(dx == 0, dz * 4 + (col & 1) * 2, 32 + dz * 6 + (dx - 1) * 2)
        key = key + row_in[0, t : t + 1, :]
        place = lax.broadcasted_iota(I32, (1, LIST), 1)
        key = jnp.where(place < count_in[0, :, t : t + 1], key, 127)
        key_buf[...] = jnp.full((8, 128), 127, I32)
        key_buf[0:1, 0:LIST] = key
        across = jnp.broadcast_to(key_buf[0:1, :], (128, 128))
        down = across.T
        lane = lax.broadcasted_iota(I32, (128, 128), 1)
        sub = lax.broadcasted_iota(I32, (128, 128), 0)

        def count(hit, axis):
            return jnp.sum(jnp.where(hit, 1, 0), axis=axis, keepdims=True)

        rank = count((across < down) | ((across == down) & (lane < sub)), 1)

        def pull(values, position):
            return jnp.sum(jnp.where(rank == position, values, 0), axis=0, keepdims=True)

        order = pull(sub, lane)
        same = jnp.where(
            (pull(down, lane) == pull(down, lane - 1)) & (lane[0:1, :] > 0), 1, 0
        )
        last = jnp.maximum(count(down <= lane, 0) - 1, 0)
        there = jnp.where(count(down == lane, 0) > 0, 1, 0)
        for r, line in enumerate((order, same, last, there)):
            tab_v[r : r + 1, :] = line
        fetch = pltpu.make_async_copy(tab_v, tab_s, tab_sem)
        fetch.start()
        fetch.wait()

    def build_adjacency(t):
        sort_entries(t)

        def add(e, total):
            total = total * tab_s[1, e].astype(F32) + vals[t, tab_s[0, e]].astype(F32)
            run[e] = total
            return total

        lax.fori_loop(0, LIST, add, jnp.zeros((TILE, TILE), F32), unroll=4)

        def summed(slot):
            return (run[tab_s[2, slot]] * tab_s[3, slot].astype(F32)).astype(BF16)

        def fill(k, carry):
            for r in range(2):
                for h in range(2):
                    near_adj[t, k, tile(r), tile(h)] = summed(k * 4 + h * 2 + r)
                for q in range(3):
                    far_adj[t, k, tile(r), tile(q)] = summed(32 + k * 6 + q * 2 + r)
            return carry

        lax.fori_loop(0, ZS, fill, 0)

    def sum_x(w, d):
        return remote(
            x_part.at[w, (x + d) % XS], x_in.at[w, d - 1],
            sum_xs.at[w, d - 1], sum_xr.at[w, d - 1], across_x[d - 1],
        )

    def sum_z(w, d):
        return remote(
            z_part.at[w, (z + d) % ZS], z_in.at[w, d - 1],
            sum_zs.at[w, d - 1], sum_zr.at[w, d - 1], across_z[d - 1],
        )

    def fin_x(w, d):
        return remote(
            done.at[w, z, x], done.at[w, z, x],
            fin_xs.at[w, d - 1], fin_xr.at[w, d - 1], across_x[d - 1],
        )

    def fin_z(w, d):
        return remote(
            done.at[w, z], done.at[w, z],
            fin_zs.at[w, d - 1], fin_zr.at[w, d - 1], across_z[d - 1],
        )

    def scatter_x(w, total):
        x_part[w] = total.astype(BF16).reshape(XS, ROWS // XS, WIDTH)
        wg_acc[w] = total
        for d in range(1, XS):
            sum_x(w, d).start()

    def scatter_z(w):
        for d in range(1, XS):
            sum_x(w, d).wait_recv()
        total = wg_acc[w, pl.ds(x * (ROWS // XS), ROWS // XS)]
        for d in range(1, XS):
            total = total + x_in[w, d - 1].astype(F32)
        for q in range(ZS):
            part = total[16 * (q // 2) : 16 * (q // 2) + 16, 128 * (q % 2) : 128 * (q % 2) + 128]
            z_own[q] = part
            z_part[w, q] = part.astype(BF16)
        for d in range(1, ZS):
            sum_z(w, d).start()

    def gather_x(w):
        for d in range(1, ZS):
            sum_z(w, d).wait_recv()
        total = z_own[z]
        for d in range(1, ZS):
            total = total + z_in[w, d - 1].astype(F32)
        done[w, z, x] = total.astype(BF16)
        for d in range(1, XS):
            fin_x(w, d).start()

    def gather_z(w):
        for d in range(1, XS):
            part = done.at[w, z, (x + XS - d) % XS]
            remote(part, part, fin_xs.at[w, d - 1], fin_xr.at[w, d - 1], x_up).wait_recv()
        for d in range(1, ZS):
            fin_z(w, d).start()

    def finish_sum(w):
        for d in range(1, ZS):
            part = done.at[w, (z + ZS - d) % ZS]
            remote(part, part, fin_zs.at[w, d - 1], fin_zr.at[w, d - 1], z_up).wait_recv()
        for q in range(ZS):
            for r in range(XS):
                top, left = r * (ROWS // XS) + 16 * (q // 2), 128 * (q % 2)
                wg_out[0, w, top : top + 16, left : left + 128] = done[w, q, r].astype(F32)
        for d in range(1, XS):
            sum_x(w, d).wait_send()
            fin_x(w, d).wait_send()
        for d in range(1, ZS):
            sum_z(w, d).wait_send()
            fin_z(w, d).wait_send()

    lent = [
        remote(preact.at[1, 1], preact_dn, lend_send.at[0], lend_recv.at[0], s_up),
        remote(weights.at[1], weights_dn, lend_send.at[1], lend_recv.at[1], s_up),
    ]

    def give_own(h):
        return remote(image_dn.at[tile(h)], full.at[2, 0, tile(h)], own_send.at[h], own_recv.at[h], s_dn)

    def give_round(p, up):
        return remote(
            image_dn.at[piece(p)], full.at[2, 7 if up else 1, piece(p)],
            (next_up if up else next_dn).at[p], full_recv.at[2, 7 if up else 1, p], dn_z_up if up else dn_z_dn,
        )

    def give_side(h):
        return remote(
            image_dn.at[pl.ds(h * TILE + RA, RC)], side.at[2, 0, late(h)],
            next_side.at[h], side_recv.at[2, 0, h], dn_side,
        )

    give_masked = remote(masked_dn, masked_in, mask_send, mask_recv, s_dn)

    def image_of(grad, live, beta, weight):
        masked32 = jnp.where(live.astype(F32) > 0, grad, 0.0)
        masked = masked32.astype(BF16)
        turned = lax.dot_general(masked, weight, (((1,), (1,)), ((), ())), preferred_element_type=F32)
        return masked, ((1.0 - beta) * masked32 + beta * turned).astype(BF16)

    def leave(n):
        source, target = (
            (hand_out.at[0], hand_hbm.at[0]),
            (init_out.at[0, 0], init_hbm.at[0, 0]),
            (init_out.at[0, 1], init_hbm.at[0, 1]),
            (wg_out.at[0, 1], wg_hbm.at[0, 1]),
            (hand_out.at[1], hand_hbm.at[1]),
            (wg_out.at[0, 0], wg_hbm.at[0, 0]),
        )[n]
        return pltpu.make_async_copy(source, target, out_sem.at[n])

    def step(i, carry):
        t = i // 2
        layer = 1 - i % 2
        beta = beta_of(section, layer)

        @pl.when(i == 0)
        def _():
            for copy in inputs[:3]:
                copy.wait()

        @pl.when(i != 2)
        def _():
            for h in range(2):
                masked, image = image_of(
                    grad_buf[tile(h)].astype(F32), preact[t, layer, tile(h)], beta, weights[layer]
                )
                masked_buf[tile(h)] = masked
                full[i, 0, tile(h)] = image
                if h == 0:
                    @pl.when(i == 0)
                    def _():
                        pl.semaphore_wait(barrier, len(peers))

                for p in range(h * PIECES // 2, (h + 1) * PIECES // 2):
                    for way in (True, False):
                        send_full(i, 0, p, way).start()
                first_side(i, h).start()

        @pl.when(i == 2)
        def _():
            for h in range(2):
                give_own(h).wait_recv()
            give_masked.wait_recv()
            masked_buf[...] = masked_in[...]

        @pl.when(i == 0)
        def _():
            for copy in lent:
                copy.start()
            for copy in inputs[3:]:
                copy.wait()
            find_needs()
            for copy in need_copies:
                copy.start()

        shown = ALPHA * full[i, 0].astype(F32)
        term = beta * lax.dot_general(
            support[t, layer], masked_buf[...], (((0,), (0,)), ((), ())),
            preferred_element_type=F32,
        )

        @pl.when(t == 0)
        def _():
            wg_acc[layer] = term

        @pl.when(t == 1)
        def _():
            scatter_x(layer, wg_acc[layer] + term)

        @pl.when(layer == 1)
        def _():
            init_out[0, t] = shown

        @pl.when(layer == 0)
        def _():
            init_out[0, t] += shown

            @pl.when(t == 0)
            def _():
                leave(1).start()

            @pl.when(t == 1)
            def _():
                leave(2).start()

        @pl.when(i == 0)
        def _():
            build_adjacency(0)
            for copy in need_copies:
                copy.wait()

        def chosen(table, q, k):
            line = table[pl.ds(t * 24 + (q - 1) * 8 + k, 1), :].astype(BF16)
            second = jnp.concatenate([line, line], axis=1)
            return 1.0 - second, second

        from_dn, from_far, from_up = (need_at.at[n] for n in range(3))

        def pass_full(k):
            for table, q, n, target, rows in (
                (from_dn, 1, 0, pick1, TILE), (from_far, 2, 1, pick2a, RA), (from_up, 3, 2, pick3, RA)
            ):
                first, second = chosen(table, q, k)
                target[k] = (
                    full[i, k, 0:rows] * first + full[i, k, TILE : TILE + rows] * second
                )
                send_far(i, k, n).start()

        def pass_side(k):
            first, second = chosen(from_up, 2, k)
            pick2c[k] = side[i, k, 0:RC] * first + side[i, k, RC : 2 * RC] * second
            send_far(i, k, 3).start()
            first, second = chosen(need, 3, k)
            far[i, k, 2 * TILE + RA : 3 * TILE] = (
                side[i, k, 0:RC] * first + side[i, k, RC : 2 * RC] * second
            )

        def product(k, near):
            adjacency, block = (near_adj[t, k], full[i, k]) if near else (far_adj[t, k], far[i, k])
            return jnp.dot(adjacency, block, preferred_element_type=F32)

        pass_full(0)

        @pl.when(i == 1)
        def _():
            build_adjacency(1)

        acc[...] = product(0, True)

        for n, arrival in enumerate(ARRIVALS):
            if len(arrival) == 1:
                (k,) = arrival
                if k == 4:
                    for copy in all_sends(i):
                        copy.wait_send()

                    @pl.when(i != 2)
                    def _():
                        for copy in [first_side(i, h) for h in range(2)] + [
                            send_full(i, 0, p, way) for p in range(PIECES) for way in (True, False)
                        ]:
                            copy.wait_send()

                    @pl.when(i == 2)
                    def _():
                        for copy in [give_own(0), give_own(1), give_side(0), give_side(1), give_masked] + [
                            give_round(p, way) for p in range(PIECES) for way in (True, False)
                        ]:
                            copy.wait_send()

                for part in range(4):
                    send_far(i, k, part).wait_recv()
                if k != 4:
                    acc[...] += product(k, False)
            else:
                c, k, h = arrival
                if c == 0:
                    remote(
                        full.at[i, k, piece(h)], full.at[i, k, piece(h)],
                        full_up.at[k, h], full_recv.at[i, k, h], z_up,
                    ).wait_recv()
                else:
                    remote(
                        side.at[i, k, late(h)], side.at[i, k, late(h)],
                        side_up.at[k, h], side_recv.at[i, k, h], z_up,
                    ).wait_recv()
                for way in moves(c, k, h):
                    (send_side if c else send_full)(i, k, h, way).start()
                taken = [a[:2] for a in ARRIVALS[: n + 1]].count((c, k))
                if taken == (2 if c else PIECES):
                    if c:
                        pass_side(k)
                    else:
                        pass_full(k)
                        acc[...] += product(k, True)

            @pl.when(t == 1)
            def _():
                if n == PHASES[0]:
                    scatter_z(layer)
                elif n == PHASES[1]:
                    gather_x(layer)
                elif n == PHASES[2]:
                    gather_z(layer)

            @pl.when(i == 3)
            def _():
                if n == PHASES[0]:
                    finish_sum(1)
                    leave(3).start()

        for h in range(2):
            spread = acc[tile(h)] + jnp.dot(
                far_adj[t, 4, tile(h)], far[i, 4], preferred_element_type=F32
            )
            grad = ((1.0 - ALPHA) * spread).astype(BF16)
            grad_buf[tile(h)] = grad

            @pl.when(i == 1)
            def _():
                if h == 0:
                    for copy in lent:
                        copy.wait()
                wraps = jnp.full((8, 128), section, I32)[0:1, 0:1] == 0
                masked, image = image_of(
                    jnp.where(wraps, grad_last[tile(h)].astype(F32), grad.astype(F32)),
                    preact_dn[tile(h)], beta_of(below, 1), weights_dn[...],
                )
                masked_dn[tile(h)] = masked
                image_dn[tile(h)] = image
                for p in range(h * PIECES // 2, (h + 1) * PIECES // 2):
                    for way in (True, False):
                        give_round(p, way).start()
                give_side(h).start()
                give_own(h).start()
                if h == 1:
                    give_masked.start()

        @pl.when(layer == 0)
        def _():
            hand_out[t, 0] = grad_buf[...]

            @pl.when(t == 0)
            def _():
                leave(0).start()

            @pl.when(t == 1)
            def _():
                leave(4).start()

        @pl.when(i == 3)
        def _():
            finish_sum(0)
            leave(5).start()
            for n in range(6):
                leave(n).wait()

        return carry

    lax.fori_loop(0, 4, step, 0)


def write_results(*refs):
    sources, targets, staged, (in_sem, out_sem) = refs[:3], refs[3:6], refs[6:9], refs[9:]
    come = [pltpu.make_async_copy(a, b, in_sem.at[n]) for n, (a, b) in enumerate(zip(sources, staged))]
    go = [pltpu.make_async_copy(a, b, out_sem.at[n]) for n, (a, b) in enumerate(zip(staged, targets))]
    for copy in come:
        copy.start()
    for first, second in zip(come, go):
        first.wait()
        second.start()
    for copy in go:
        copy.wait()


def shards(grad_in, grad_last, support, preact, weights, tile_vals, tile_row, tile_col, tile_count):
    anywhere = pl.BlockSpec(memory_space=pl.ANY)
    shapes = (
        jax.ShapeDtypeStruct((2, 1, ROWS, WIDTH), BF16),
        jax.ShapeDtypeStruct((1, 2, ROWS, WIDTH), F32),
        jax.ShapeDtypeStruct((1, 2, WIDTH, WIDTH), F32),
    )
    results = pl.pallas_call(
        kernel,
        out_shape=shapes,
        in_specs=[anywhere] * 9,
        out_specs=(anywhere,) * 3,
        scratch_shapes=[pltpu.VMEM(s.shape, s.dtype) for s in shapes]
        + [
            pltpu.VMEM((1, 2, LIST), I32),
            pltpu.VMEM((1, 2, LIST), I32),
            pltpu.VMEM((1, 1, 2), I32),
            pltpu.VMEM((ROWS, WIDTH), BF16),
            pltpu.VMEM((2, 2, ROWS, WIDTH), BF16),
            pltpu.VMEM((2, 2, ROWS, WIDTH), BF16),
            pltpu.VMEM((2, WIDTH, WIDTH), BF16),
            pltpu.VMEM((ROWS, WIDTH), BF16),
            pltpu.VMEM((WIDTH, WIDTH), BF16),
            pltpu.VMEM((ROWS, WIDTH), BF16),
            pltpu.VMEM((ROWS, WIDTH), BF16),
            pltpu.VMEM((ROWS, WIDTH), BF16),
            pltpu.VMEM((2, WIDTH, WIDTH), F32),
            pltpu.VMEM((2, XS, ROWS // XS, WIDTH), BF16),
            pltpu.VMEM((2, XS - 1, ROWS // XS, WIDTH), BF16),
            pltpu.VMEM((ZS, 16, 128), F32),
            pltpu.VMEM((2, ZS, 16, 128), BF16),
            pltpu.VMEM((2, ZS - 1, 16, 128), BF16),
            pltpu.VMEM((2, ZS, XS, 16, 128), BF16),
            pltpu.VMEM((2, LIST, TILE, TILE), BF16),
            pltpu.VMEM((8, 128), I32),
            pltpu.VMEM((8, 128), I32),
            pltpu.SMEM((8, 128), I32),
            pltpu.VMEM((48, 128), F32),
            pltpu.VMEM((3, 48, 128), F32),
            pltpu.VMEM((LIST, TILE, TILE), F32),
            pltpu.VMEM((2, ZS, ROWS, 2 * TILE), BF16),
            pltpu.VMEM((2, ZS, ROWS, 3 * TILE), BF16),
            pltpu.VMEM((4, ZS, ROWS, WIDTH), BF16),
            pltpu.VMEM((4, ZS, 2 * RC, WIDTH), BF16),
            pltpu.VMEM((4, ZS, 3 * TILE, WIDTH), BF16),
            pltpu.VMEM((ZS, TILE, WIDTH), BF16),
            pltpu.VMEM((ZS, RA, WIDTH), BF16),
            pltpu.VMEM((ZS, RA, WIDTH), BF16),
            pltpu.VMEM((ZS, RC, WIDTH), BF16),
            pltpu.VMEM((ROWS, WIDTH), BF16),
            pltpu.VMEM((ROWS, WIDTH), BF16),
            pltpu.VMEM((ROWS, WIDTH), F32),
            pltpu.SemaphoreType.DMA((8,)),
            pltpu.SemaphoreType.DMA((6,)),
            pltpu.SemaphoreType.DMA((2,)),
            pltpu.SemaphoreType.DMA,
            pltpu.SemaphoreType.DMA((3,)),
            pltpu.SemaphoreType.DMA((3,)),
            pltpu.SemaphoreType.DMA((ZS, PIECES)),
            pltpu.SemaphoreType.DMA((ZS, PIECES)),
            pltpu.SemaphoreType.DMA((4, ZS, PIECES)),
            pltpu.SemaphoreType.DMA((2,)),
            pltpu.SemaphoreType.DMA((ZS, 2)),
            pltpu.SemaphoreType.DMA((ZS, 2)),
            pltpu.SemaphoreType.DMA((4, ZS, 2)),
            pltpu.SemaphoreType.DMA((4, ZS)),
            pltpu.SemaphoreType.DMA((4, 4, ZS)),
            pltpu.SemaphoreType.DMA((2,)),
            pltpu.SemaphoreType.DMA((2,)),
            pltpu.SemaphoreType.DMA((2,)),
            pltpu.SemaphoreType.DMA((2,)),
            pltpu.SemaphoreType.DMA,
            pltpu.SemaphoreType.DMA,
            pltpu.SemaphoreType.DMA((PIECES,)),
            pltpu.SemaphoreType.DMA((PIECES,)),
            pltpu.SemaphoreType.DMA((2,)),
        ]
        + [pltpu.SemaphoreType.DMA((2, n - 1)) for n in (XS, XS, ZS, ZS, ZS, ZS, XS, XS)],
        compiler_params=pltpu.CompilerParams(
            collective_id=0, has_side_effects=True, vmem_limit_bytes=60 * 1024 * 1024
        ),
    )(grad_in, grad_last, support, preact, weights, tile_vals, tile_row, tile_col, jnp.swapaxes(tile_count, 1, 2))
    return pl.pallas_call(
        write_results,
        out_shape=shapes,
        in_specs=[anywhere] * 3,
        out_specs=(anywhere,) * 3,
        scratch_shapes=[pltpu.VMEM(s.shape, s.dtype) for s in shapes]
        + [pltpu.SemaphoreType.DMA((3,)), pltpu.SemaphoreType.DMA((3,))],
    )(*results)


def solution(mesh):
    return jax.shard_map(
        shards,
        mesh=mesh,
        in_specs=(
            P("section", "rows", None),
            P("rows", None),
            P("section", None, None, "rows", None),
            P("section", None, None, "rows", None),
            P("section", None, None, None),
            P("section", None, "rows", None, None),
            P("section", None, "rows"),
            P("section", None, "rows"),
            P("section", None, "rows"),
        ),
        out_specs=(
            P(None, "section", "rows", None),
            P("section", None, "rows", None),
            P("section", None, None, None),
        ),
        check_vma=False,
    )
```

```python
import jax
import jax.numpy as jnp
from jax import lax
from jax.experimental import pallas as pl
from jax.experimental.pallas import tpu as pltpu
from jax.sharding import PartitionSpec as P

ALPHA = 0.1
BETA_SCALE = 0.5
MESH = pl.DeviceIdType.MESH

SECTIONS = 8
XS = 4
ZS = 8
TILE = 128
WIDTH = 256
ROWS = 256
LIST = 96
RA = 64
PIECES = 4
RC = TILE - RA
LATE_TERM = 36
PHASES = (9, 19, 28, 42, 47)
ARRIVALS = (
    (1, 0, 0), (0, 7, 0), (0, 1, 0), (1, 0, 1), (0, 7, 1), (0, 1, 1), (0, 7, 2), (0, 1, 2), (0, 7, 3), (0, 1, 3),
    (1, 7, 0), (1, 1, 0), (0, 6, 0), (0, 2, 0), (1, 7, 1), (1, 1, 1), (0, 6, 1), (0, 2, 1), (0, 6, 2), (0, 2, 2),
    (0, 6, 3), (0, 2, 3), (1, 6, 0), (1, 2, 0), (0,), (0, 5, 0), (0, 3, 0), (1, 6, 1), (1, 2, 1), (0, 5, 1),
    (0, 3, 1), (0, 5, 2), (0, 3, 2), (0, 5, 3), (0, 3, 3), (1, 5, 0), (1, 3, 0), (0, 4, 0), (1, 3, 1), (1, 5, 1),
    (7,), (1,), (0, 4, 1), (0, 4, 2), (0, 4, 3), (1, 4, 0), (1, 4, 1), (6,), (2,), (5,), (3,), (4,),
)
F32 = jnp.float32
BF16 = jnp.bfloat16
I32 = jnp.int32


def kernel(
    grad_hbm, last_hbm, support_hbm, preact_hbm, weights_hbm, vals_hbm, row_hbm, col_hbm, count_hbm,
    hand_hbm, init_hbm, wg_hbm,
    hand_out, init_out, wg_out,
    row_in, col_in, count_in, grad_last, support, preact, weights, preact_dn, weights_dn, masked_dn, image_dn,
    masked_in, wg_acc, x_part, x_in, z_own, z_part, z_in, done, zz_part, zz_in, xx_own, xx_part, xx_in,
    vals, key_buf, tab_v, tab_s, need, need_at, run, near_adj, far_adj,
    full, side, far, pick1, pick2a, pick3, pick2c, grad_buf, masked_buf, acc,
    in_sem, out_sem, vals_sem, tab_sem, need_send, need_recv, full_up, full_dn, full_recv,
    side_first, side_up, side_dn, side_recv, far_send, far_recv,
    lend_send, lend_recv, own_send, own_recv, mask_send, mask_recv, next_up, next_dn, next_side, zz_send, zz_recv, xx_send, xx_recv, sum_xs, sum_xr, sum_zs, sum_zr, fin_zs, fin_zr, fin_xs, fin_xr,
):
    section = lax.axis_index("section")
    me = lax.axis_index("rows")
    x = me // ZS
    z = me % ZS

    def at(sec, xx, zz):
        return (sec, xx * ZS + zz)

    across_x = [at(section, (x + d) % XS, z) for d in range(1, XS)]
    across_z = [at(section, x, (z + d) % ZS) for d in range(1, ZS)]
    x_up, x_far, x_dn = across_x
    z_up, z_dn = across_z[0], across_z[-1]
    above, below = (section + 1) % SECTIONS, (section + SECTIONS - 1) % SECTIONS
    s_up, s_dn = at(above, x, z), at(below, x, z)
    dn_side = at(below, (x + 1) % XS, z)
    dn_z_up, dn_z_dn = at(below, x, (z + 1) % ZS), at(below, x, (z + ZS - 1) % ZS)
    up_peers = [at(above, (x + XS - 1) % XS, z), at(above, x, (z + ZS - 1) % ZS), at(above, x, (z + 1) % ZS)]

    barrier = pltpu.get_barrier_semaphore()
    peers = across_x + across_z + [s_up, s_dn, dn_side, dn_z_up, dn_z_dn] + up_peers
    for peer in peers:
        pl.semaphore_signal(barrier, inc=1, device_id=peer, device_id_type=MESH)

    inputs = [
        pltpu.make_async_copy(source, target, in_sem.at[n])
        for n, (source, target) in enumerate((
            (grad_hbm.at[0], grad_buf),
            (preact_hbm.at[0], preact),
            (weights_hbm.at[0], weights),
            (col_hbm, col_in),
            (row_hbm, row_in),
            (count_hbm, count_in),
            (support_hbm.at[0], support),
            (last_hbm, grad_last),
        ))
    ] + [pltpu.make_async_copy(vals_hbm.at[0, t], vals.at[t], vals_sem.at[t]) for t in range(2)]
    for copy in inputs:
        copy.start()

    def remote(src, dst, send, recv, device):
        return pltpu.make_async_remote_copy(
            src_ref=src, dst_ref=dst, send_sem=send, recv_sem=recv,
            device_id=device, device_id_type=MESH,
        )

    def tile(h):
        return pl.ds(h * TILE, TILE)

    def piece(p):
        return pl.ds(p * (ROWS // PIECES), ROWS // PIECES)

    def late(h):
        return pl.ds(h * RC, RC)

    def send_full(i, k, h, up):
        k_to = (k + (7 if up else 1)) % ZS
        return remote(
            full.at[i, k, piece(h)], full.at[i, k_to, piece(h)],
            (full_up if up else full_dn).at[k, h], full_recv.at[i, k_to, h], z_up if up else z_dn,
        )

    def send_side(i, k, h, up):
        k_to = (k + (7 if up else 1)) % ZS
        return remote(
            side.at[i, k, late(h)], side.at[i, k_to, late(h)],
            (side_up if up else side_dn).at[k, h], side_recv.at[i, k_to, h], z_up if up else z_dn,
        )

    def first_side(i, h):
        return remote(
            full.at[i, 0, pl.ds(h * TILE + RA, RC)], side.at[i, 0, late(h)],
            side_first.at[h], side_recv.at[i, 0, h], x_up,
        )

    def send_far(i, k, n):
        source, start, size, device = (
            (pick1.at[k], 0, TILE, x_dn),
            (pick2a.at[k], TILE, RA, x_far),
            (pick3.at[k], 2 * TILE, RA, x_up),
            (pick2c.at[k], TILE + RA, RC, x_up),
        )[n]
        return remote(
            source, far.at[i, k, pl.ds(start, size)], far_send.at[n, k], far_recv.at[i, n, k], device
        )

    def moves(c, k, h):
        first = h < (1 if c else PIECES // 2)
        up = k in (0, 7, 6) or (k == 5 and first)
        dn = k in (0, 1, 2) or (k == 3 and not first)
        return [way for way, goes in ((True, up), (False, dn)) if goes]

    need_copies = [
        remote(need, need_at.at[n], need_send.at[n], need_recv.at[n], device)
        for n, device in enumerate((x_up, x_far, x_dn))
    ]

    def all_sends(i):
        copies = []
        for k in range(ZS):
            if k:
                copies += [send_full(i, k, p, way) for p in range(PIECES) for way in moves(0, k, p)]
            copies += [send_side(i, k, h, way) for h in range(2) for way in moves(1, k, h)]
            copies += [send_far(i, k, n) for n in range(4)]
        return copies

    def beta_of(place, layer):
        depth = (2 * place + layer + 1).astype(F32)
        return jnp.log(BETA_SCALE / jnp.full((8, 128), depth, F32) + 1.0)[0:1, 0:1]

    def find_needs():
        slot = lax.broadcasted_iota(I32, (24, LIST), 0)
        owner = ((x + 1 + (slot >> 3)) & 3) * ZS + ((z + slot) & 7)
        for t in range(2):
            col = jnp.broadcast_to(col_in[0, t : t + 1, :], (24, LIST))
            second = jnp.where((col >> 1) == owner, (col & 1).astype(F32), 0.0)
            need[t * 24 : (t + 1) * 24, :] = jnp.broadcast_to(
                jnp.max(second, axis=1, keepdims=True), (24, 128)
            )

    def sort_entries(t):
        col = col_in[0, t : t + 1, :]
        owner = col >> 1
        dx = ((owner >> 3) - x) & 3
        dz = ((owner & 7) - z) & 7
        key = jnp.where(dx == 0, dz * 4 + (col & 1) * 2, 32 + dz * 6 + (dx - 1) * 2)
        key = key + row_in[0, t : t + 1, :]
        place = lax.broadcasted_iota(I32, (1, LIST), 1)
        key = jnp.where(place < count_in[0, :, t : t + 1], key, 127)
        key_buf[...] = jnp.full((8, 128), 127, I32)
        key_buf[0:1, 0:LIST] = key
        across = jnp.broadcast_to(key_buf[0:1, :], (128, 128))
        down = across.T
        lane = lax.broadcasted_iota(I32, (128, 128), 1)
        sub = lax.broadcasted_iota(I32, (128, 128), 0)

        def count(hit, axis):
            return jnp.sum(jnp.where(hit, 1, 0), axis=axis, keepdims=True)

        rank = count((across < down) | ((across == down) & (lane < sub)), 1)

        def pull(values, position):
            return jnp.sum(jnp.where(rank == position, values, 0), axis=0, keepdims=True)

        order = pull(sub, lane)
        same = jnp.where(
            (pull(down, lane) == pull(down, lane - 1)) & (lane[0:1, :] > 0), 1, 0
        )
        last = jnp.maximum(count(down <= lane, 0) - 1, 0)
        there = jnp.where(count(down == lane, 0) > 0, 1, 0)
        for r, line in enumerate((order, same, last, there)):
            tab_v[r : r + 1, :] = line
        fetch = pltpu.make_async_copy(tab_v, tab_s, tab_sem)
        fetch.start()
        fetch.wait()

    def build_adjacency(t):
        sort_entries(t)

        def add(e, total):
            total = total * tab_s[1, e].astype(F32) + vals[t, tab_s[0, e]].astype(F32)
            run[e] = total
            return total

        lax.fori_loop(0, LIST, add, jnp.zeros((TILE, TILE), F32), unroll=4)

        def summed(slot):
            return (run[tab_s[2, slot]] * tab_s[3, slot].astype(F32)).astype(BF16)

        def fill(k, carry):
            for r in range(2):
                for h in range(2):
                    near_adj[t, k, tile(r), tile(h)] = summed(k * 4 + h * 2 + r)
                for q in range(3):
                    far_adj[t, k, tile(r), tile(q)] = summed(32 + k * 6 + q * 2 + r)
            return carry

        lax.fori_loop(0, ZS, fill, 0)

    def sum_x(w, d):
        return remote(
            x_part.at[w, (x + d) % XS], x_in.at[w, d - 1],
            sum_xs.at[w, d - 1], sum_xr.at[w, d - 1], across_x[d - 1],
        )

    def sum_z(w, d):
        return remote(
            z_part.at[w, (z + d) % ZS], z_in.at[w, d - 1],
            sum_zs.at[w, d - 1], sum_zr.at[w, d - 1], across_z[d - 1],
        )

    def fin_x(w, d):
        return remote(
            done.at[w, z, x], done.at[w, z, x],
            fin_xs.at[w, d - 1], fin_xr.at[w, d - 1], across_x[d - 1],
        )

    def fin_z(w, d):
        return remote(
            done.at[w, z], done.at[w, z],
            fin_zs.at[w, d - 1], fin_zr.at[w, d - 1], across_z[d - 1],
        )

    def scatter_x(w, total):
        x_part[w] = total.astype(BF16).reshape(XS, ROWS // XS, WIDTH)
        wg_acc[w] = total
        for d in range(1, XS):
            sum_x(w, d).start()

    def scatter_z(w):
        for d in range(1, XS):
            sum_x(w, d).wait_recv()
        total = wg_acc[w, pl.ds(x * (ROWS // XS), ROWS // XS)]
        for d in range(1, XS):
            total = total + x_in[w, d - 1].astype(F32)
        for q in range(ZS):
            part = total[16 * (q // 2) : 16 * (q // 2) + 16, 128 * (q % 2) : 128 * (q % 2) + 128]
            z_own[q] = part
            z_part[w, q] = part.astype(BF16)
        for d in range(1, ZS):
            sum_z(w, d).start()

    def sum_zz(d):
        return remote(
            zz_part.at[(z + d) % ZS], zz_in.at[d - 1], zz_send.at[d - 1], zz_recv.at[d - 1], across_z[d - 1]
        )

    def sum_xx(d):
        return remote(
            xx_part.at[(x + d) % XS], xx_in.at[d - 1], xx_send.at[d - 1], xx_recv.at[d - 1], across_x[d - 1]
        )

    def scatter_zz():
        zz_part[...] = wg_acc[1].astype(BF16).reshape(ZS, ROWS // ZS, WIDTH)
        for d in range(1, ZS):
            sum_zz(d).start()

    def scatter_xx():
        for d in range(1, ZS):
            sum_zz(d).wait()
        total = wg_acc[1, pl.ds(z * (ROWS // ZS), ROWS // ZS)]
        for d in range(1, ZS):
            total = total + zz_in[d - 1].astype(F32)
        for r in range(XS):
            part = total[16 * (r // 2) : 16 * (r // 2) + 16, 128 * (r % 2) : 128 * (r % 2) + 128]
            xx_own[r] = part
            xx_part[r] = part.astype(BF16)
        for d in range(1, XS):
            sum_xx(d).start()

    def gather_x(w):
        if w:
            for d in range(1, XS):
                sum_xx(d).wait()
            total = xx_own[x]
            for d in range(1, XS):
                total = total + xx_in[d - 1].astype(F32)
        else:
            for d in range(1, ZS):
                sum_z(w, d).wait_recv()
            total = z_own[z]
            for d in range(1, ZS):
                total = total + z_in[w, d - 1].astype(F32)
        done[w, z, x] = total.astype(BF16)
        for d in range(1, XS):
            fin_x(w, d).start()

    def gather_z(w):
        for d in range(1, XS):
            part = done.at[w, z, (x + XS - d) % XS]
            remote(part, part, fin_xs.at[w, d - 1], fin_xr.at[w, d - 1], x_up).wait_recv()
        for d in range(1, ZS):
            fin_z(w, d).start()

    def finish_sum(w):
        for d in range(1, ZS):
            part = done.at[w, (z + ZS - d) % ZS]
            remote(part, part, fin_zs.at[w, d - 1], fin_zr.at[w, d - 1], z_up).wait_recv()
        for q in range(ZS):
            for r in range(XS):
                if w:
                    top, left = q * (ROWS // ZS) + 16 * (r // 2), 128 * (r % 2)
                else:
                    top, left = r * (ROWS // XS) + 16 * (q // 2), 128 * (q % 2)
                wg_out[0, w, top : top + 16, left : left + 128] = done[w, q, r].astype(F32)
        for d in range(1, XS):
            fin_x(w, d).wait_send()
            if w == 0:
                sum_x(w, d).wait_send()
        for d in range(1, ZS):
            fin_z(w, d).wait_send()
            if w == 0:
                sum_z(w, d).wait_send()

    lent = [
        remote(preact.at[1, 1], preact_dn, lend_send.at[0], lend_recv.at[0], s_up),
        remote(weights.at[1], weights_dn, lend_send.at[1], lend_recv.at[1], s_up),
    ]

    def give_own(h):
        return remote(image_dn.at[tile(h)], full.at[2, 0, tile(h)], own_send.at[h], own_recv.at[h], s_dn)

    def give_round(p, up):
        return remote(
            image_dn.at[piece(p)], full.at[2, 7 if up else 1, piece(p)],
            (next_up if up else next_dn).at[p], full_recv.at[2, 7 if up else 1, p], dn_z_up if up else dn_z_dn,
        )

    def give_side(h):
        return remote(
            image_dn.at[pl.ds(h * TILE + RA, RC)], side.at[2, 0, late(h)],
            next_side.at[h], side_recv.at[2, 0, h], dn_side,
        )

    give_masked = remote(masked_dn, masked_in, mask_send, mask_recv, s_dn)

    def image_of(grad, live, beta, weight):
        masked32 = jnp.where(live.astype(F32) > 0, grad, 0.0)
        masked = masked32.astype(BF16)
        turned = lax.dot_general(masked, weight, (((1,), (1,)), ((), ())), preferred_element_type=F32)
        return masked, ((1.0 - beta) * masked32 + beta * turned).astype(BF16)

    def leave(n):
        source, target = (
            (hand_out.at[0], hand_hbm.at[0]),
            (init_out.at[0, 0], init_hbm.at[0, 0]),
            (init_out.at[0, 1], init_hbm.at[0, 1]),
            (wg_out.at[0, 1], wg_hbm.at[0, 1]),
            (hand_out.at[1], hand_hbm.at[1]),
            (wg_out.at[0, 0], wg_hbm.at[0, 0]),
        )[n]
        return pltpu.make_async_copy(source, target, out_sem.at[n])

    def step(i, carry):
        t = i // 2
        layer = 1 - i % 2
        beta = beta_of(section, layer)

        @pl.when(i == 0)
        def _():
            for copy in inputs[:3]:
                copy.wait()

        @pl.when(i != 2)
        def _():
            for h in range(2):
                masked, image = image_of(
                    grad_buf[tile(h)].astype(F32), preact[t, layer, tile(h)], beta, weights[layer]
                )
                masked_buf[tile(h)] = masked
                full[i, 0, tile(h)] = image
                if h == 0:
                    @pl.when(i == 0)
                    def _():
                        pl.semaphore_wait(barrier, len(peers))

                for p in range(h * PIECES // 2, (h + 1) * PIECES // 2):
                    for way in (True, False):
                        send_full(i, 0, p, way).start()
                first_side(i, h).start()

        @pl.when(i == 2)
        def _():
            for h in range(2):
                give_own(h).wait_recv()

        @pl.when(i == 0)
        def _():
            for copy in lent:
                copy.start()
            for copy in inputs[3:6]:
                copy.wait()
            find_needs()
            for copy in need_copies:
                copy.start()
            for copy in inputs[6:]:
                copy.wait()

        shown = ALPHA * full[i, 0].astype(F32)
        def weight_term():
            term = beta * lax.dot_general(
                support[t, layer], masked_buf[...], (((0,), (0,)), ((), ())),
                preferred_element_type=F32,
            )

            @pl.when(t == 0)
            def _():
                wg_acc[layer] = term

            @pl.when(i == 2)
            def _():
                wg_acc[1] += term

            @pl.when(i == 3)
            def _():
                scatter_x(0, wg_acc[0] + term)

        @pl.when(i != 2)
        def _():
            weight_term()

        @pl.when(layer == 1)
        def _():
            init_out[0, t] = shown

        @pl.when(layer == 0)
        def _():
            init_out[0, t] += shown

            @pl.when(t == 0)
            def _():
                leave(1).start()

            @pl.when(t == 1)
            def _():
                leave(2).start()

        @pl.when(i == 0)
        def _():
            build_adjacency(0)
            for copy in need_copies:
                copy.wait()

        def chosen(table, q, k):
            line = table[pl.ds(t * 24 + (q - 1) * 8 + k, 1), :].astype(BF16)
            second = jnp.concatenate([line, line], axis=1)
            return 1.0 - second, second

        from_dn, from_far, from_up = (need_at.at[n] for n in range(3))

        def pass_full(k):
            for table, q, n, target, rows in (
                (from_dn, 1, 0, pick1, TILE), (from_far, 2, 1, pick2a, RA), (from_up, 3, 2, pick3, RA)
            ):
                first, second = chosen(table, q, k)
                target[k] = (
                    full[i, k, 0:rows] * first + full[i, k, TILE : TILE + rows] * second
                )
                send_far(i, k, n).start()

        def pass_side(k):
            first, second = chosen(from_up, 2, k)
            pick2c[k] = side[i, k, 0:RC] * first + side[i, k, RC : 2 * RC] * second
            send_far(i, k, 3).start()
            first, second = chosen(need, 3, k)
            far[i, k, 2 * TILE + RA : 3 * TILE] = (
                side[i, k, 0:RC] * first + side[i, k, RC : 2 * RC] * second
            )

        def product(k, near):
            adjacency, block = (near_adj[t, k], full[i, k]) if near else (far_adj[t, k], far[i, k])
            return jnp.dot(adjacency, block, preferred_element_type=F32)

        pass_full(0)

        @pl.when(i == 1)
        def _():
            build_adjacency(1)

        acc[...] = product(0, True)

        for n, arrival in enumerate(ARRIVALS):
            if len(arrival) == 1:
                (k,) = arrival
                if k == 4:
                    for copy in all_sends(i):
                        copy.wait_send()

                    @pl.when(i != 2)
                    def _():
                        for copy in [first_side(i, h) for h in range(2)] + [
                            send_full(i, 0, p, way) for p in range(PIECES) for way in (True, False)
                        ]:
                            copy.wait_send()

                    @pl.when(i == 2)
                    def _():
                        for copy in [give_own(0), give_own(1), give_side(0), give_side(1), give_masked] + [
                            give_round(p, way) for p in range(PIECES) for way in (True, False)
                        ]:
                            copy.wait_send()

                for part in range(4):
                    send_far(i, k, part).wait_recv()
                if k != 4:
                    acc[...] += product(k, False)
            else:
                c, k, h = arrival
                if c == 0:
                    remote(
                        full.at[i, k, piece(h)], full.at[i, k, piece(h)],
                        full_up.at[k, h], full_recv.at[i, k, h], z_up,
                    ).wait_recv()
                else:
                    remote(
                        side.at[i, k, late(h)], side.at[i, k, late(h)],
                        side_up.at[k, h], side_recv.at[i, k, h], z_up,
                    ).wait_recv()
                for way in moves(c, k, h):
                    (send_side if c else send_full)(i, k, h, way).start()
                taken = [a[:2] for a in ARRIVALS[: n + 1]].count((c, k))
                if taken == (2 if c else PIECES):
                    if c:
                        pass_side(k)
                    else:
                        pass_full(k)
                        acc[...] += product(k, True)

            if n == LATE_TERM:
                @pl.when(i == 2)
                def _():
                    give_masked.wait_recv()
                    masked_buf[...] = masked_in[...]
                    weight_term()

            @pl.when(i == 2)
            def _():
                if n == PHASES[3]:
                    scatter_zz()

            @pl.when(i == 3)
            def _():
                if n == PHASES[0]:
                    scatter_xx()
                elif n == PHASES[1]:
                    scatter_z(0)
                elif n == PHASES[2]:
                    gather_x(1)
                elif n == PHASES[3]:
                    gather_z(1)
                    gather_x(0)
                elif n == PHASES[4]:
                    gather_z(0)

        for h in range(2):
            spread = acc[tile(h)] + jnp.dot(
                far_adj[t, 4, tile(h)], far[i, 4], preferred_element_type=F32
            )
            grad = ((1.0 - ALPHA) * spread).astype(BF16)
            grad_buf[tile(h)] = grad

            @pl.when(i == 1)
            def _():
                if h == 0:
                    for copy in lent:
                        copy.wait()
                wraps = jnp.full((8, 128), section, I32)[0:1, 0:1] == 0
                masked, image = image_of(
                    jnp.where(wraps, grad_last[tile(h)].astype(F32), grad.astype(F32)),
                    preact_dn[tile(h)], beta_of(below, 1), weights_dn[...],
                )
                masked_dn[tile(h)] = masked
                image_dn[tile(h)] = image
                for p in range(h * PIECES // 2, (h + 1) * PIECES // 2):
                    for way in (True, False):
                        give_round(p, way).start()
                give_side(h).start()
                give_own(h).start()
                if h == 1:
                    give_masked.start()

        @pl.when(layer == 0)
        def _():
            hand_out[t, 0] = grad_buf[...]

            @pl.when(t == 0)
            def _():
                leave(0).start()

            @pl.when(t == 1)
            def _():
                leave(4).start()

        @pl.when(i == 3)
        def _():
            finish_sum(1)
            leave(3).start()
            finish_sum(0)
            leave(5).start()
            for n in range(6):
                leave(n).wait()

        return carry

    lax.fori_loop(0, 4, step, 0)


def write_results(*refs):
    sources, targets, staged, (in_sem, out_sem) = refs[:3], refs[3:6], refs[6:9], refs[9:]
    come = [pltpu.make_async_copy(a, b, in_sem.at[n]) for n, (a, b) in enumerate(zip(sources, staged))]
    go = [pltpu.make_async_copy(a, b, out_sem.at[n]) for n, (a, b) in enumerate(zip(staged, targets))]
    for copy in come:
        copy.start()
    for first, second in zip(come, go):
        first.wait()
        second.start()
    for copy in go:
        copy.wait()


def shards(grad_in, grad_last, support, preact, weights, tile_vals, tile_row, tile_col, tile_count):
    anywhere = pl.BlockSpec(memory_space=pl.ANY)
    shapes = (
        jax.ShapeDtypeStruct((2, 1, ROWS, WIDTH), BF16),
        jax.ShapeDtypeStruct((1, 2, ROWS, WIDTH), F32),
        jax.ShapeDtypeStruct((1, 2, WIDTH, WIDTH), F32),
    )
    results = pl.pallas_call(
        kernel,
        out_shape=shapes,
        in_specs=[anywhere] * 9,
        out_specs=(anywhere,) * 3,
        scratch_shapes=[pltpu.VMEM(s.shape, s.dtype) for s in shapes]
        + [
            pltpu.VMEM((1, 2, LIST), I32),
            pltpu.VMEM((1, 2, LIST), I32),
            pltpu.VMEM((1, 1, 2), I32),
            pltpu.VMEM((ROWS, WIDTH), BF16),
            pltpu.VMEM((2, 2, ROWS, WIDTH), BF16),
            pltpu.VMEM((2, 2, ROWS, WIDTH), BF16),
            pltpu.VMEM((2, WIDTH, WIDTH), BF16),
            pltpu.VMEM((ROWS, WIDTH), BF16),
            pltpu.VMEM((WIDTH, WIDTH), BF16),
            pltpu.VMEM((ROWS, WIDTH), BF16),
            pltpu.VMEM((ROWS, WIDTH), BF16),
            pltpu.VMEM((ROWS, WIDTH), BF16),
            pltpu.VMEM((2, WIDTH, WIDTH), F32),
            pltpu.VMEM((2, XS, ROWS // XS, WIDTH), BF16),
            pltpu.VMEM((2, XS - 1, ROWS // XS, WIDTH), BF16),
            pltpu.VMEM((ZS, 16, 128), F32),
            pltpu.VMEM((2, ZS, 16, 128), BF16),
            pltpu.VMEM((2, ZS - 1, 16, 128), BF16),
            pltpu.VMEM((2, ZS, XS, 16, 128), BF16),
            pltpu.VMEM((ZS, ROWS // ZS, WIDTH), BF16),
            pltpu.VMEM((ZS - 1, ROWS // ZS, WIDTH), BF16),
            pltpu.VMEM((XS, 16, 128), F32),
            pltpu.VMEM((XS, 16, 128), BF16),
            pltpu.VMEM((XS - 1, 16, 128), BF16),
            pltpu.VMEM((2, LIST, TILE, TILE), BF16),
            pltpu.VMEM((8, 128), I32),
            pltpu.VMEM((8, 128), I32),
            pltpu.SMEM((8, 128), I32),
            pltpu.VMEM((48, 128), F32),
            pltpu.VMEM((3, 48, 128), F32),
            pltpu.VMEM((LIST, TILE, TILE), F32),
            pltpu.VMEM((2, ZS, ROWS, 2 * TILE), BF16),
            pltpu.VMEM((2, ZS, ROWS, 3 * TILE), BF16),
            pltpu.VMEM((4, ZS, ROWS, WIDTH), BF16),
            pltpu.VMEM((4, ZS, 2 * RC, WIDTH), BF16),
            pltpu.VMEM((4, ZS, 3 * TILE, WIDTH), BF16),
            pltpu.VMEM((ZS, TILE, WIDTH), BF16),
            pltpu.VMEM((ZS, RA, WIDTH), BF16),
            pltpu.VMEM((ZS, RA, WIDTH), BF16),
            pltpu.VMEM((ZS, RC, WIDTH), BF16),
            pltpu.VMEM((ROWS, WIDTH), BF16),
            pltpu.VMEM((ROWS, WIDTH), BF16),
            pltpu.VMEM((ROWS, WIDTH), F32),
            pltpu.SemaphoreType.DMA((8,)),
            pltpu.SemaphoreType.DMA((6,)),
            pltpu.SemaphoreType.DMA((2,)),
            pltpu.SemaphoreType.DMA,
            pltpu.SemaphoreType.DMA((3,)),
            pltpu.SemaphoreType.DMA((3,)),
            pltpu.SemaphoreType.DMA((ZS, PIECES)),
            pltpu.SemaphoreType.DMA((ZS, PIECES)),
            pltpu.SemaphoreType.DMA((4, ZS, PIECES)),
            pltpu.SemaphoreType.DMA((2,)),
            pltpu.SemaphoreType.DMA((ZS, 2)),
            pltpu.SemaphoreType.DMA((ZS, 2)),
            pltpu.SemaphoreType.DMA((4, ZS, 2)),
            pltpu.SemaphoreType.DMA((4, ZS)),
            pltpu.SemaphoreType.DMA((4, 4, ZS)),
            pltpu.SemaphoreType.DMA((2,)),
            pltpu.SemaphoreType.DMA((2,)),
            pltpu.SemaphoreType.DMA((2,)),
            pltpu.SemaphoreType.DMA((2,)),
            pltpu.SemaphoreType.DMA,
            pltpu.SemaphoreType.DMA,
            pltpu.SemaphoreType.DMA((PIECES,)),
            pltpu.SemaphoreType.DMA((PIECES,)),
            pltpu.SemaphoreType.DMA((2,)),
            pltpu.SemaphoreType.DMA((ZS - 1,)),
            pltpu.SemaphoreType.DMA((ZS - 1,)),
            pltpu.SemaphoreType.DMA((XS - 1,)),
            pltpu.SemaphoreType.DMA((XS - 1,)),
        ]
        + [pltpu.SemaphoreType.DMA((2, n - 1)) for n in (XS, XS, ZS, ZS, ZS, ZS, XS, XS)],
        compiler_params=pltpu.CompilerParams(
            collective_id=0, has_side_effects=True, vmem_limit_bytes=60 * 1024 * 1024
        ),
    )(grad_in, grad_last, support, preact, weights, tile_vals, tile_row, tile_col, jnp.swapaxes(tile_count, 1, 2))
    return pl.pallas_call(
        write_results,
        out_shape=shapes,
        in_specs=[anywhere] * 3,
        out_specs=(anywhere,) * 3,
        scratch_shapes=[pltpu.VMEM(s.shape, s.dtype) for s in shapes]
        + [pltpu.SemaphoreType.DMA((3,)), pltpu.SemaphoreType.DMA((3,))],
    )(*results)


def solution(mesh):
    return jax.shard_map(
        shards,
        mesh=mesh,
        in_specs=(
            P("section", "rows", None),
            P("rows", None),
            P("section", None, None, "rows", None),
            P("section", None, None, "rows", None),
            P("section", None, None, None),
            P("section", None, "rows", None, None),
            P("section", None, "rows"),
            P("section", None, "rows"),
            P("section", None, "rows"),
        ),
        out_specs=(
            P(None, "section", "rows", None),
            P("section", None, "rows", None),
            P("section", None, None, None),
        ),
        check_vma=False,
    )
```

```python
import jax
import jax.numpy as jnp
from jax import lax
from jax.experimental import pallas as pl
from jax.experimental.pallas import tpu as pltpu
from jax.sharding import PartitionSpec as P

ALPHA = 0.1
BETA_SCALE = 0.5
MESH = pl.DeviceIdType.MESH

SECTIONS = 8
XS = 4
ZS = 8
TILE = 128
WIDTH = 256
ROWS = 256
LIST = 96
RA = 64
PIECES = 4
RC = TILE - RA
LATE_TERM = 36
PHASES = (9, 19, 28, 42, 47)
ARRIVALS = (
    (1, 0, 0), (0, 7, 0), (0, 1, 0), (1, 0, 1), (0, 7, 1), (0, 1, 1), (0, 7, 2), (0, 1, 2), (0, 7, 3), (0, 1, 3),
    (1, 7, 0), (1, 1, 0), (0, 6, 0), (0, 2, 0), (1, 7, 1), (1, 1, 1), (0, 6, 1), (0, 2, 1), (0, 6, 2), (0, 2, 2),
    (0, 6, 3), (0, 2, 3), (1, 6, 0), (1, 2, 0), (0,), (0, 5, 0), (0, 3, 0), (1, 6, 1), (1, 2, 1), (0, 5, 1),
    (0, 3, 1), (0, 5, 2), (0, 3, 2), (0, 5, 3), (0, 3, 3), (1, 5, 0), (1, 3, 0), (0, 4, 0), (1, 3, 1), (1, 5, 1),
    (7,), (1,), (0, 4, 1), (0, 4, 2), (0, 4, 3), (1, 4, 0), (1, 4, 1), (6,), (2,), (5,), (3,), (4,),
)
F32 = jnp.float32
BF16 = jnp.bfloat16
I32 = jnp.int32


def kernel(
    grad_hbm, last_hbm, support_hbm, preact_hbm, weights_hbm, vals_hbm, row_hbm, col_hbm, count_hbm,
    hand_hbm, init_hbm, wg_hbm,
    hand_out, init_out, wg_out,
    row_in, col_in, count_in, grad_last, support, preact, weights, preact_dn, weights_dn, masked_dn, image_dn,
    masked_in, wg_acc, x_part, x_in, z_own, z_part, z_in, done, zz_part, zz_in, xx_own, xx_part, xx_in,
    vals, key_buf, tab_v, tab_s, need, need_at, run, near_adj, far_adj,
    full, side, far, pick1, pick2a, pick3, pick2c, grad_buf, masked_buf, acc,
    in_sem, out_sem, vals_sem, tab_sem, need_send, need_recv, full_up, full_dn, full_recv,
    side_first, side_up, side_dn, side_recv, far_send, far_recv,
    lend_send, lend_recv, own_send, own_recv, mask_send, mask_recv, next_up, next_dn, next_side, zz_send, zz_recv, xx_send, xx_recv, sum_xs, sum_xr, sum_zs, sum_zr, fin_zs, fin_zr, fin_xs, fin_xr,
):
    section = lax.axis_index("section")
    me = lax.axis_index("rows")
    x = me // ZS
    z = me % ZS

    def at(sec, xx, zz):
        return (sec, xx * ZS + zz)

    across_x = [at(section, (x + d) % XS, z) for d in range(1, XS)]
    across_z = [at(section, x, (z + d) % ZS) for d in range(1, ZS)]
    x_up, x_far, x_dn = across_x
    z_up, z_dn = across_z[0], across_z[-1]
    above, below = (section + 1) % SECTIONS, (section + SECTIONS - 1) % SECTIONS
    s_up, s_dn = at(above, x, z), at(below, x, z)
    dn_side = at(below, (x + 1) % XS, z)
    dn_z_up, dn_z_dn = at(below, x, (z + 1) % ZS), at(below, x, (z + ZS - 1) % ZS)
    up_peers = [at(above, (x + XS - 1) % XS, z), at(above, x, (z + ZS - 1) % ZS), at(above, x, (z + 1) % ZS)]

    barrier = pltpu.get_barrier_semaphore()
    peers = across_x + across_z + [s_up, s_dn, dn_side, dn_z_up, dn_z_dn] + up_peers
    for peer in peers:
        pl.semaphore_signal(barrier, inc=1, device_id=peer, device_id_type=MESH)

    inputs = [
        pltpu.make_async_copy(source, target, in_sem.at[n])
        for n, (source, target) in enumerate((
            (grad_hbm.at[0], grad_buf),
            (preact_hbm.at[0], preact),
            (weights_hbm.at[0], weights),
            (col_hbm, col_in),
            (row_hbm, row_in),
            (count_hbm, count_in),
            (support_hbm.at[0], support),
            (last_hbm, grad_last),
        ))
    ] + [pltpu.make_async_copy(vals_hbm.at[0, t], vals.at[t], vals_sem.at[t]) for t in range(2)]
    for copy in inputs:
        copy.start()

    def remote(src, dst, send, recv, device):
        return pltpu.make_async_remote_copy(
            src_ref=src, dst_ref=dst, send_sem=send, recv_sem=recv,
            device_id=device, device_id_type=MESH,
        )

    def tile(h):
        return pl.ds(h * TILE, TILE)

    def piece(p):
        return pl.ds(p * (ROWS // PIECES), ROWS // PIECES)

    def late(h):
        return pl.ds(h * RC, RC)

    def send_full(i, k, h, up):
        k_to = (k + (7 if up else 1)) % ZS
        return remote(
            full.at[i, k, piece(h)], full.at[i, k_to, piece(h)],
            (full_up if up else full_dn).at[k, h], full_recv.at[i, k_to, h], z_up if up else z_dn,
        )

    def send_side(i, k, h, up):
        k_to = (k + (7 if up else 1)) % ZS
        return remote(
            side.at[i, k, late(h)], side.at[i, k_to, late(h)],
            (side_up if up else side_dn).at[k, h], side_recv.at[i, k_to, h], z_up if up else z_dn,
        )

    def first_side(i, h):
        return remote(
            full.at[i, 0, pl.ds(h * TILE + RA, RC)], side.at[i, 0, late(h)],
            side_first.at[h], side_recv.at[i, 0, h], x_up,
        )

    def send_far(i, k, n):
        source, start, size, device = (
            (pick1.at[k], 0, TILE, x_dn),
            (pick2a.at[k], TILE, RA, x_far),
            (pick3.at[k], 2 * TILE, RA, x_up),
            (pick2c.at[k], TILE + RA, RC, x_up),
        )[n]
        return remote(
            source, far.at[i, k, pl.ds(start, size)], far_send.at[n, k], far_recv.at[i, n, k], device
        )

    def moves(c, k, h):
        first = h < (1 if c else PIECES // 2)
        up = k in (0, 7, 6) or (k == 5 and first)
        dn = k in (0, 1, 2) or (k == 3 and not first)
        return [way for way, goes in ((True, up), (False, dn)) if goes]

    need_copies = [
        remote(need, need_at.at[n], need_send.at[n], need_recv.at[n], device)
        for n, device in enumerate((x_up, x_far, x_dn))
    ]

    def all_sends(i):
        copies = []
        for k in range(ZS):
            if k:
                copies += [send_full(i, k, p, way) for p in range(PIECES) for way in moves(0, k, p)]
            copies += [send_side(i, k, h, way) for h in range(2) for way in moves(1, k, h)]
            copies += [send_far(i, k, n) for n in range(4)]
        return copies

    def beta_of(place, layer):
        depth = (2 * place + layer + 1).astype(F32)
        return jnp.log(BETA_SCALE / jnp.full((8, 128), depth, F32) + 1.0)[0:1, 0:1]

    def find_needs():
        slot = lax.broadcasted_iota(I32, (24, LIST), 0)
        owner = ((x + 1 + (slot >> 3)) & 3) * ZS + ((z + slot) & 7)
        for t in range(2):
            col = jnp.broadcast_to(col_in[0, t : t + 1, :], (24, LIST))
            second = jnp.where((col >> 1) == owner, (col & 1).astype(F32), 0.0)
            need[t * 24 : (t + 1) * 24, :] = jnp.broadcast_to(
                jnp.max(second, axis=1, keepdims=True), (24, 128)
            )

    def sort_entries(t):
        col = col_in[0, t : t + 1, :]
        owner = col >> 1
        dx = ((owner >> 3) - x) & 3
        dz = ((owner & 7) - z) & 7
        key = jnp.where(dx == 0, dz * 4 + (col & 1) * 2, 32 + dz * 6 + (dx - 1) * 2)
        key = key + row_in[0, t : t + 1, :]
        place = lax.broadcasted_iota(I32, (1, LIST), 1)
        key = jnp.where(place < count_in[0, :, t : t + 1], key, 127)
        key_buf[...] = jnp.full((8, 128), 127, I32)
        key_buf[0:1, 0:LIST] = key
        across = jnp.broadcast_to(key_buf[0:1, :], (128, 128))
        down = across.T
        lane = lax.broadcasted_iota(I32, (128, 128), 1)
        sub = lax.broadcasted_iota(I32, (128, 128), 0)

        def count(hit, axis):
            return jnp.sum(jnp.where(hit, 1, 0), axis=axis, keepdims=True)

        rank = count((across < down) | ((across == down) & (lane < sub)), 1)

        def pull(values, position):
            return jnp.sum(jnp.where(rank == position, values, 0), axis=0, keepdims=True)

        order = pull(sub, lane)
        same = jnp.where(
            (pull(down, lane) == pull(down, lane - 1)) & (lane[0:1, :] > 0), 1, 0
        )
        last = jnp.maximum(count(down <= lane, 0) - 1, 0)
        there = jnp.where(count(down == lane, 0) > 0, 1, 0)
        for r, line in enumerate((order, same, last, there)):
            tab_v[r : r + 1, :] = line
        fetch = pltpu.make_async_copy(tab_v, tab_s, tab_sem)
        fetch.start()
        fetch.wait()

    def build_adjacency(t):
        sort_entries(t)

        def add(e, total):
            total = total * tab_s[1, e].astype(F32) + vals[t, tab_s[0, e]].astype(F32)
            run[e] = total
            return total

        lax.fori_loop(0, LIST, add, jnp.zeros((TILE, TILE), F32), unroll=4)

        def summed(slot):
            return (run[tab_s[2, slot]] * tab_s[3, slot].astype(F32)).astype(BF16)

        def fill(k, carry):
            for r in range(2):
                for h in range(2):
                    near_adj[t, k, tile(r), tile(h)] = summed(k * 4 + h * 2 + r)
                for q in range(3):
                    far_adj[t, k, tile(r), tile(q)] = summed(32 + k * 6 + q * 2 + r)
            return carry

        lax.fori_loop(0, ZS, fill, 0)

    def sum_x(w, d):
        return remote(
            x_part.at[w, (x + d) % XS], x_in.at[w, d - 1],
            sum_xs.at[w, d - 1], sum_xr.at[w, d - 1], across_x[d - 1],
        )

    def sum_z(w, d):
        return remote(
            z_part.at[w, (z + d) % ZS], z_in.at[w, d - 1],
            sum_zs.at[w, d - 1], sum_zr.at[w, d - 1], across_z[d - 1],
        )

    def fin_x(w, d):
        return remote(
            done.at[w, z, x], done.at[w, z, x],
            fin_xs.at[w, d - 1], fin_xr.at[w, d - 1], across_x[d - 1],
        )

    def fin_z(w, d):
        return remote(
            done.at[w, z], done.at[w, z],
            fin_zs.at[w, d - 1], fin_zr.at[w, d - 1], across_z[d - 1],
        )

    def scatter_x(w, total):
        x_part[w] = total.astype(BF16).reshape(XS, ROWS // XS, WIDTH)
        wg_acc[w] = total
        for d in range(1, XS):
            sum_x(w, d).start()

    def scatter_z(w):
        for d in range(1, XS):
            sum_x(w, d).wait_recv()
        total = wg_acc[w, pl.ds(x * (ROWS // XS), ROWS // XS)]
        for d in range(1, XS):
            total = total + x_in[w, d - 1].astype(F32)
        for q in range(ZS):
            part = total[16 * (q // 2) : 16 * (q // 2) + 16, 128 * (q % 2) : 128 * (q % 2) + 128]
            z_own[q] = part
            z_part[w, q] = part.astype(BF16)
        for d in range(1, ZS):
            sum_z(w, d).start()

    def sum_zz(d):
        return remote(
            zz_part.at[(z + d) % ZS], zz_in.at[d - 1], zz_send.at[d - 1], zz_recv.at[d - 1], across_z[d - 1]
        )

    def sum_xx(d):
        return remote(
            xx_part.at[(x + d) % XS], xx_in.at[d - 1], xx_send.at[d - 1], xx_recv.at[d - 1], across_x[d - 1]
        )

    def scatter_zz():
        zz_part[...] = wg_acc[1].astype(BF16).reshape(ZS, ROWS // ZS, WIDTH)
        for d in range(1, ZS):
            sum_zz(d).start()

    def scatter_xx():
        for d in range(1, ZS):
            sum_zz(d).wait()
        total = wg_acc[1, pl.ds(z * (ROWS // ZS), ROWS // ZS)]
        for d in range(1, ZS):
            total = total + zz_in[d - 1].astype(F32)
        for r in range(XS):
            part = total[16 * (r // 2) : 16 * (r // 2) + 16, 128 * (r % 2) : 128 * (r % 2) + 128]
            xx_own[r] = part
            xx_part[r] = part.astype(BF16)
        for d in range(1, XS):
            sum_xx(d).start()

    def gather_x(w):
        if w:
            for d in range(1, XS):
                sum_xx(d).wait()
            total = xx_own[x]
            for d in range(1, XS):
                total = total + xx_in[d - 1].astype(F32)
        else:
            for d in range(1, ZS):
                sum_z(w, d).wait_recv()
            total = z_own[z]
            for d in range(1, ZS):
                total = total + z_in[w, d - 1].astype(F32)
        done[w, z, x] = total.astype(BF16)
        for d in range(1, XS):
            fin_x(w, d).start()

    def gather_z(w):
        for d in range(1, XS):
            part = done.at[w, z, (x + XS - d) % XS]
            remote(part, part, fin_xs.at[w, d - 1], fin_xr.at[w, d - 1], x_up).wait_recv()
        for d in range(1, ZS):
            fin_z(w, d).start()

    def finish_sum(w):
        for d in range(1, ZS):
            part = done.at[w, (z + ZS - d) % ZS]
            remote(part, part, fin_zs.at[w, d - 1], fin_zr.at[w, d - 1], z_up).wait_recv()
        for q in range(ZS):
            for r in range(XS):
                if w:
                    top, left = q * (ROWS // ZS) + 16 * (r // 2), 128 * (r % 2)
                else:
                    top, left = r * (ROWS // XS) + 16 * (q // 2), 128 * (q % 2)
                wg_out[0, w, top : top + 16, left : left + 128] = done[w, q, r].astype(F32)
        for d in range(1, XS):
            fin_x(w, d).wait_send()
            if w == 0:
                sum_x(w, d).wait_send()
        for d in range(1, ZS):
            fin_z(w, d).wait_send()
            if w == 0:
                sum_z(w, d).wait_send()

    lent = [
        remote(preact.at[1, 1], preact_dn, lend_send.at[0], lend_recv.at[0], s_up),
        remote(weights.at[1], weights_dn, lend_send.at[1], lend_recv.at[1], s_up),
    ]

    def give_own(h):
        return remote(image_dn.at[tile(h)], full.at[2, 0, tile(h)], own_send.at[h], own_recv.at[h], s_dn)

    def give_round(p, up):
        return remote(
            image_dn.at[piece(p)], full.at[2, 7 if up else 1, piece(p)],
            (next_up if up else next_dn).at[p], full_recv.at[2, 7 if up else 1, p], dn_z_up if up else dn_z_dn,
        )

    def give_side(h):
        return remote(
            image_dn.at[pl.ds(h * TILE + RA, RC)], side.at[2, 0, late(h)],
            next_side.at[h], side_recv.at[2, 0, h], dn_side,
        )

    give_masked = remote(masked_dn, masked_in, mask_send, mask_recv, s_dn)

    def image_of(grad, live, beta, weight):
        masked32 = jnp.where(live.astype(F32) > 0, grad, 0.0)
        masked = masked32.astype(BF16)
        turned = lax.dot_general(masked, weight, (((1,), (1,)), ((), ())), preferred_element_type=F32)
        return masked, ((1.0 - beta) * masked32 + beta * turned).astype(BF16)

    def leave(n):
        source, target = (
            (hand_out.at[0], hand_hbm.at[0]),
            (init_out.at[0, 0], init_hbm.at[0, 0]),
            (init_out.at[0, 1], init_hbm.at[0, 1]),
            (wg_out.at[0, 1], wg_hbm.at[0, 1]),
            (hand_out.at[1], hand_hbm.at[1]),
            (wg_out.at[0, 0], wg_hbm.at[0, 0]),
        )[n]
        return pltpu.make_async_copy(source, target, out_sem.at[n])

    def step(i, carry):
        t = i // 2
        layer = 1 - i % 2
        beta = beta_of(section, layer)

        @pl.when(i == 0)
        def _():
            for copy in inputs[:3]:
                copy.wait()

        @pl.when(i != 2)
        def _():
            for h in range(2):
                masked, image = image_of(
                    grad_buf[tile(h)].astype(F32), preact[t, layer, tile(h)], beta, weights[layer]
                )
                masked_buf[tile(h)] = masked
                full[i, 0, tile(h)] = image
                if h == 0:
                    @pl.when(i == 0)
                    def _():
                        pl.semaphore_wait(barrier, len(peers))

                for p in range(h * PIECES // 2, (h + 1) * PIECES // 2):
                    for way in (True, False):
                        send_full(i, 0, p, way).start()
                first_side(i, h).start()

        @pl.when(i == 2)
        def _():
            for h in range(2):
                give_own(h).wait_recv()

        @pl.when(i == 0)
        def _():
            for copy in lent:
                copy.start()
            for copy in inputs[3:6]:
                copy.wait()
            find_needs()
            for copy in need_copies:
                copy.start()
            for copy in inputs[6:]:
                copy.wait()

        shown = ALPHA * full[i, 0].astype(F32)
        def weight_term():
            term = beta * lax.dot_general(
                support[t, layer], masked_buf[...], (((0,), (0,)), ((), ())),
                preferred_element_type=F32,
            )

            @pl.when(t == 0)
            def _():
                wg_acc[layer] = term

            @pl.when(i == 2)
            def _():
                wg_acc[1] += term

            @pl.when(i == 3)
            def _():
                scatter_x(0, wg_acc[0] + term)

        @pl.when(i != 2)
        def _():
            weight_term()

        @pl.when(layer == 1)
        def _():
            init_out[0, t] = shown

        @pl.when(layer == 0)
        def _():
            init_out[0, t] += shown

            @pl.when(t == 0)
            def _():
                leave(1).start()

            @pl.when(t == 1)
            def _():
                leave(2).start()

        @pl.when(i == 0)
        def _():
            build_adjacency(0)
            for copy in need_copies:
                copy.wait()

        def chosen(table, q, k):
            line = table[pl.ds(t * 24 + (q - 1) * 8 + k, 1), :].astype(BF16)
            second = jnp.concatenate([line, line], axis=1)
            return 1.0 - second, second

        from_dn, from_far, from_up = (need_at.at[n] for n in range(3))

        def pass_full(k):
            for table, q, n, target, rows in (
                (from_far, 2, 1, pick2a, RA), (from_dn, 1, 0, pick1, TILE), (from_up, 3, 2, pick3, RA)
            ):
                first, second = chosen(table, q, k)
                target[k] = (
                    full[i, k, 0:rows] * first + full[i, k, TILE : TILE + rows] * second
                )
                send_far(i, k, n).start()

        def pass_side(k):
            first, second = chosen(from_up, 2, k)
            pick2c[k] = side[i, k, 0:RC] * first + side[i, k, RC : 2 * RC] * second
            send_far(i, k, 3).start()
            first, second = chosen(need, 3, k)
            far[i, k, 2 * TILE + RA : 3 * TILE] = (
                side[i, k, 0:RC] * first + side[i, k, RC : 2 * RC] * second
            )

        def product(k, near):
            adjacency, block = (near_adj[t, k], full[i, k]) if near else (far_adj[t, k], far[i, k])
            return jnp.dot(adjacency, block, preferred_element_type=F32)

        pass_full(0)

        @pl.when(i == 1)
        def _():
            build_adjacency(1)

        acc[...] = product(0, True)

        for n, arrival in enumerate(ARRIVALS):
            if len(arrival) == 1:
                (k,) = arrival
                if k == 4:
                    for copy in all_sends(i):
                        copy.wait_send()

                    @pl.when(i != 2)
                    def _():
                        for copy in [first_side(i, h) for h in range(2)] + [
                            send_full(i, 0, p, way) for p in range(PIECES) for way in (True, False)
                        ]:
                            copy.wait_send()

                    @pl.when(i == 2)
                    def _():
                        for copy in [give_own(0), give_own(1), give_side(0), give_side(1), give_masked] + [
                            give_round(p, way) for p in range(PIECES) for way in (True, False)
                        ]:
                            copy.wait_send()

                for part in range(4):
                    send_far(i, k, part).wait_recv()
                if k != 4:
                    acc[...] += product(k, False)
            else:
                c, k, h = arrival
                if c == 0:
                    remote(
                        full.at[i, k, piece(h)], full.at[i, k, piece(h)],
                        full_up.at[k, h], full_recv.at[i, k, h], z_up,
                    ).wait_recv()
                else:
                    remote(
                        side.at[i, k, late(h)], side.at[i, k, late(h)],
                        side_up.at[k, h], side_recv.at[i, k, h], z_up,
                    ).wait_recv()
                for way in moves(c, k, h):
                    (send_side if c else send_full)(i, k, h, way).start()
                taken = [a[:2] for a in ARRIVALS[: n + 1]].count((c, k))
                if taken == (2 if c else PIECES):
                    if c:
                        pass_side(k)
                    else:
                        pass_full(k)
                        acc[...] += product(k, True)

            if n == LATE_TERM:
                @pl.when(i == 2)
                def _():
                    give_masked.wait_recv()
                    masked_buf[...] = masked_in[...]
                    weight_term()

            @pl.when(i == 2)
            def _():
                if n == PHASES[3]:
                    scatter_zz()

            @pl.when(i == 3)
            def _():
                if n == PHASES[0]:
                    scatter_xx()
                elif n == PHASES[1]:
                    scatter_z(0)
                elif n == PHASES[2]:
                    gather_x(1)
                elif n == PHASES[3]:
                    gather_z(1)
                    gather_x(0)
                elif n == PHASES[4]:
                    gather_z(0)

        for h in range(2):
            spread = acc[tile(h)] + jnp.dot(
                far_adj[t, 4, tile(h)], far[i, 4], preferred_element_type=F32
            )
            grad = ((1.0 - ALPHA) * spread).astype(BF16)
            grad_buf[tile(h)] = grad

            @pl.when(i == 1)
            def _():
                if h == 0:
                    for copy in lent:
                        copy.wait()
                wraps = jnp.full((8, 128), section, I32)[0:1, 0:1] == 0
                masked, image = image_of(
                    jnp.where(wraps, grad_last[tile(h)].astype(F32), grad.astype(F32)),
                    preact_dn[tile(h)], beta_of(below, 1), weights_dn[...],
                )
                masked_dn[tile(h)] = masked
                image_dn[tile(h)] = image
                for p in range(h * PIECES // 2, (h + 1) * PIECES // 2):
                    for way in (True, False):
                        give_round(p, way).start()
                give_side(h).start()
                give_own(h).start()
                if h == 1:
                    give_masked.start()

        @pl.when(layer == 0)
        def _():
            hand_out[t, 0] = grad_buf[...]

            @pl.when(t == 0)
            def _():
                leave(0).start()

            @pl.when(t == 1)
            def _():
                leave(4).start()

        @pl.when(i == 3)
        def _():
            finish_sum(1)
            leave(3).start()
            finish_sum(0)
            leave(5).start()
            for n in range(6):
                leave(n).wait()

        return carry

    lax.fori_loop(0, 4, step, 0)


def write_results(*refs):
    sources, targets, staged, (in_sem, out_sem) = refs[:3], refs[3:6], refs[6:9], refs[9:]
    come = [pltpu.make_async_copy(a, b, in_sem.at[n]) for n, (a, b) in enumerate(zip(sources, staged))]
    go = [pltpu.make_async_copy(a, b, out_sem.at[n]) for n, (a, b) in enumerate(zip(staged, targets))]
    for copy in come:
        copy.start()
    for first, second in zip(come, go):
        first.wait()
        second.start()
    for copy in go:
        copy.wait()


def shards(grad_in, grad_last, support, preact, weights, tile_vals, tile_row, tile_col, tile_count):
    anywhere = pl.BlockSpec(memory_space=pl.ANY)
    shapes = (
        jax.ShapeDtypeStruct((2, 1, ROWS, WIDTH), BF16),
        jax.ShapeDtypeStruct((1, 2, ROWS, WIDTH), F32),
        jax.ShapeDtypeStruct((1, 2, WIDTH, WIDTH), F32),
    )
    results = pl.pallas_call(
        kernel,
        out_shape=shapes,
        in_specs=[anywhere] * 9,
        out_specs=(anywhere,) * 3,
        scratch_shapes=[pltpu.VMEM(s.shape, s.dtype) for s in shapes]
        + [
            pltpu.VMEM((1, 2, LIST), I32),
            pltpu.VMEM((1, 2, LIST), I32),
            pltpu.VMEM((1, 1, 2), I32),
            pltpu.VMEM((ROWS, WIDTH), BF16),
            pltpu.VMEM((2, 2, ROWS, WIDTH), BF16),
            pltpu.VMEM((2, 2, ROWS, WIDTH), BF16),
            pltpu.VMEM((2, WIDTH, WIDTH), BF16),
            pltpu.VMEM((ROWS, WIDTH), BF16),
            pltpu.VMEM((WIDTH, WIDTH), BF16),
            pltpu.VMEM((ROWS, WIDTH), BF16),
            pltpu.VMEM((ROWS, WIDTH), BF16),
            pltpu.VMEM((ROWS, WIDTH), BF16),
            pltpu.VMEM((2, WIDTH, WIDTH), F32),
            pltpu.VMEM((2, XS, ROWS // XS, WIDTH), BF16),
            pltpu.VMEM((2, XS - 1, ROWS // XS, WIDTH), BF16),
            pltpu.VMEM((ZS, 16, 128), F32),
            pltpu.VMEM((2, ZS, 16, 128), BF16),
            pltpu.VMEM((2, ZS - 1, 16, 128), BF16),
            pltpu.VMEM((2, ZS, XS, 16, 128), BF16),
            pltpu.VMEM((ZS, ROWS // ZS, WIDTH), BF16),
            pltpu.VMEM((ZS - 1, ROWS // ZS, WIDTH), BF16),
            pltpu.VMEM((XS, 16, 128), F32),
            pltpu.VMEM((XS, 16, 128), BF16),
            pltpu.VMEM((XS - 1, 16, 128), BF16),
            pltpu.VMEM((2, LIST, TILE, TILE), BF16),
            pltpu.VMEM((8, 128), I32),
            pltpu.VMEM((8, 128), I32),
            pltpu.SMEM((8, 128), I32),
            pltpu.VMEM((48, 128), F32),
            pltpu.VMEM((3, 48, 128), F32),
            pltpu.VMEM((LIST, TILE, TILE), F32),
            pltpu.VMEM((2, ZS, ROWS, 2 * TILE), BF16),
            pltpu.VMEM((2, ZS, ROWS, 3 * TILE), BF16),
            pltpu.VMEM((4, ZS, ROWS, WIDTH), BF16),
            pltpu.VMEM((4, ZS, 2 * RC, WIDTH), BF16),
            pltpu.VMEM((4, ZS, 3 * TILE, WIDTH), BF16),
            pltpu.VMEM((ZS, TILE, WIDTH), BF16),
            pltpu.VMEM((ZS, RA, WIDTH), BF16),
            pltpu.VMEM((ZS, RA, WIDTH), BF16),
            pltpu.VMEM((ZS, RC, WIDTH), BF16),
            pltpu.VMEM((ROWS, WIDTH), BF16),
            pltpu.VMEM((ROWS, WIDTH), BF16),
            pltpu.VMEM((ROWS, WIDTH), F32),
            pltpu.SemaphoreType.DMA((8,)),
            pltpu.SemaphoreType.DMA((6,)),
            pltpu.SemaphoreType.DMA((2,)),
            pltpu.SemaphoreType.DMA,
            pltpu.SemaphoreType.DMA((3,)),
            pltpu.SemaphoreType.DMA((3,)),
            pltpu.SemaphoreType.DMA((ZS, PIECES)),
            pltpu.SemaphoreType.DMA((ZS, PIECES)),
            pltpu.SemaphoreType.DMA((4, ZS, PIECES)),
            pltpu.SemaphoreType.DMA((2,)),
            pltpu.SemaphoreType.DMA((ZS, 2)),
            pltpu.SemaphoreType.DMA((ZS, 2)),
            pltpu.SemaphoreType.DMA((4, ZS, 2)),
            pltpu.SemaphoreType.DMA((4, ZS)),
            pltpu.SemaphoreType.DMA((4, 4, ZS)),
            pltpu.SemaphoreType.DMA((2,)),
            pltpu.SemaphoreType.DMA((2,)),
            pltpu.SemaphoreType.DMA((2,)),
            pltpu.SemaphoreType.DMA((2,)),
            pltpu.SemaphoreType.DMA,
            pltpu.SemaphoreType.DMA,
            pltpu.SemaphoreType.DMA((PIECES,)),
            pltpu.SemaphoreType.DMA((PIECES,)),
            pltpu.SemaphoreType.DMA((2,)),
            pltpu.SemaphoreType.DMA((ZS - 1,)),
            pltpu.SemaphoreType.DMA((ZS - 1,)),
            pltpu.SemaphoreType.DMA((XS - 1,)),
            pltpu.SemaphoreType.DMA((XS - 1,)),
        ]
        + [pltpu.SemaphoreType.DMA((2, n - 1)) for n in (XS, XS, ZS, ZS, ZS, ZS, XS, XS)],
        compiler_params=pltpu.CompilerParams(
            collective_id=0, has_side_effects=True, vmem_limit_bytes=60 * 1024 * 1024
        ),
    )(grad_in, grad_last, support, preact, weights, tile_vals, tile_row, tile_col, jnp.swapaxes(tile_count, 1, 2))
    return pl.pallas_call(
        write_results,
        out_shape=shapes,
        in_specs=[anywhere] * 3,
        out_specs=(anywhere,) * 3,
        scratch_shapes=[pltpu.VMEM(s.shape, s.dtype) for s in shapes]
        + [pltpu.SemaphoreType.DMA((3,)), pltpu.SemaphoreType.DMA((3,))],
    )(*results)


def solution(mesh):
    return jax.shard_map(
        shards,
        mesh=mesh,
        in_specs=(
            P("section", "rows", None),
            P("rows", None),
            P("section", None, None, "rows", None),
            P("section", None, None, "rows", None),
            P("section", None, None, None),
            P("section", None, "rows", None, None),
            P("section", None, "rows"),
            P("section", None, "rows"),
            P("section", None, "rows"),
        ),
        out_specs=(
            P(None, "section", "rows", None),
            P("section", None, "rows", None),
            P("section", None, None, None),
        ),
        check_vma=False,
    )
```
